128 devices in a mesh: il: 16 (over x, z), xl: 8 (over y, core).
Axes of the slice: x: 4, y: 4, z: 4, core: 2. Of those that a mesh axis runs over, the one named last changes fastest.
Arguments:
- traces: bfloat16 [65536, 1536], P(('il', 'xl')), may hold values from -6 to 6
- fold_ids: int32 [64, 128, 4], P('il', 'xl'), may hold values from 0 to 65535, as said below
- fold_counts: int32 [64, 128], P('il', 'xl'), may hold values from 2 to 4
- conv1_w: bfloat16 [8, 64], replicated, may hold values from -2 to 2
- conv2_w: bfloat16 [512, 256], replicated, may hold values from -0.25 to 0.25
- conv3_w: bfloat16 [768, 256], replicated, may hold values from -0.21875 to 0.21875
- conv4_w: bfloat16 [768, 256], replicated, may hold values from -0.21875 to 0.21875
- lateral_w: float32 [256, 9], P('xl'), may hold values from -2 to 2
Outputs:
- encoded: bfloat16 [96, 256, 64, 128], P('il', 'xl')
The draws below stay inside these ranges and needn't reach their ends.
Inputs may be any that keep to these rules, and one draw needn't show every extreme that they name: `fold_ids`: among the slots of one device's 4 x 16 bins, at most 4 name traces of any one shard (ids k * 512 to (k + 1) * 512 - 1, the shard of device k in il+xl order), and some shard is named exactly 4 times. Dead slots (index at or beyond the bin's count) also hold valid ids.
All inputs are finite; a program needn't handle non-finite values.
Results may differ from the reference program's by a relative error of at most 0.014.
Values may be sent and summed in bfloat16 or wider, within the bound.
A program may use at most 192 MiB of HBM per device.

```python
import jax
import jax.numpy as jnp
import numpy as np
from jax import lax

NT = 1536
C1 = 64
C2 = 256
FOLD = 4
BI = 4
BX = 16
TR_DEV = 512
NIL = 64
NXL = 128
TRACES = 65536
CAP = 4
T2 = 96


def draw_fold_ids(key, part):
    il_tiles = NIL // BI
    xl_tiles = NXL // BX
    device_total = il_tiles * xl_tiles
    slot_total = BI * BX * FOLD
    pattern = np.array([CAP, 3 * CAP // 4, CAP // 4, 0], dtype=np.int32)
    repeats = jnp.array(np.tile(pattern, device_total // 4), dtype=jnp.int32)

    def one_owner(owner):
        owner_key = jax.random.fold_in(key, owner)
        key_order, key_slots, key_rows = jax.random.split(owner_key, 3)
        order = jax.random.permutation(key_order, device_total).astype(jnp.int32)
        sources_sorted = jnp.repeat(order, repeats, total_repeat_length=slot_total)
        sources = sources_sorted[jax.random.permutation(key_slots, slot_total)]
        local_rows = jax.random.randint(key_rows, (slot_total,), 0, TR_DEV, dtype=jnp.int32)
        return (sources * TR_DEV + local_rows).astype(jnp.int32)
    owners = jax.vmap(one_owner)(jnp.arange(device_total, dtype=jnp.int32))
    tiles = owners.reshape(il_tiles, xl_tiles, BI, BX, FOLD)
    return tiles.transpose(0, 2, 1, 3, 4).reshape(NIL, NXL, FOLD)


def set_ends(values, key, least, high):
    shape = values.shape
    index_at = [jax.random.randint(jax.random.fold_in(key, axis), (), 0, shape[axis]) for axis in range(len(shape))]
    values = values.at[tuple(index_at)].set(least)
    longest = shape.index(max(shape))
    index_at[longest] = (index_at[longest] + 1) % shape[longest]
    return values.at[tuple(index_at)].set(high)


def block_scale(rng, extent, cuts, smallest, largest):
    def one(dim, shards_of):
        steps = jax.random.uniform(jax.random.fold_in(jax.random.fold_in(rng, 6), dim), (shards_of,), jnp.float32, smallest / len(cuts), largest / len(cuts))
        return jnp.repeat(jnp.exp(steps), extent[dim] // shards_of).reshape((-1,) + (1,) * (len(extent) - dim - 1))

    loudness = one(*cuts[0])
    for cut in cuts[1:]:
        loudness = loudness * one(*cut)
    return loudness


def bell_draw(stream_key, dims, width, reach, cuts=(), kind=jnp.bfloat16):
    gain = block_scale(stream_key, dims, cuts, -0.22, 0.18) if cuts else 1.0
    entries = jax.random.normal(stream_key, dims, jnp.float32) * width * gain
    return jnp.minimum(jnp.maximum(entries, -reach), reach).astype(kind)


def setup_inputs(seed: int = 0) -> dict:
    key_list = jax.random.split(jax.random.key(seed), 9)
    traces = bell_draw(key_list[0], (TRACES, NT), 1.0, 6.0, ((0, 128),))
    fold_ids = draw_fold_ids(jax.random.fold_in(key_list[8], 71), 0)
    fold_counts = set_ends(jax.random.randint(key_list[2], (NIL, NXL), 2, FOLD + 1), jax.random.fold_in(key_list[2], 1), 2, FOLD).astype(jnp.int32)
    conv1_w = bell_draw(key_list[3], (8, C1), 8 ** -0.5, 2.0)
    conv2_w = bell_draw(key_list[4], (8 * C1, C2), (8 * C1) ** -0.5, 0.25)
    conv3_w = bell_draw(key_list[5], (3 * C2, C2), (3 * C2) ** -0.5, 0.21875)
    conv4_w = bell_draw(key_list[6], (3 * C2, C2), (3 * C2) ** -0.5, 0.21875)
    lateral_w = bell_draw(key_list[7], (C2, 9), 9 ** -0.5, 2.0, ((0, 8),), jnp.float32)
    return {"traces": traces, "fold_ids": fold_ids, "fold_counts": fold_counts, "conv1_w": conv1_w, "conv2_w": conv2_w, "conv3_w": conv3_w, "conv4_w": conv4_w, "lateral_w": lateral_w}


def strided_conv(inputs, weight):
    batch_rows, length, channels = inputs.shape
    padded = jnp.pad(inputs, ((0, 0), (4, 0), (0, 0)))
    earlier = padded[:, :length].reshape(batch_rows * (length // 4), 4 * channels)
    current = padded[:, 4:].reshape(batch_rows * (length // 4), 4 * channels)
    result = jnp.dot(earlier, weight[:4 * channels], preferred_element_type=jnp.float32)
    result = result + jnp.dot(current, weight[4 * channels:], preferred_element_type=jnp.float32)
    return result.reshape(batch_rows, length // 4, weight.shape[1])


def centred_conv(inputs, weight):
    batch_rows, length, channels = inputs.shape
    padded = jnp.pad(inputs, ((0, 0), (1, 1), (0, 0)))
    result = jnp.zeros((batch_rows * length, weight.shape[1]), jnp.float32)
    for offset in range(3):
        window = padded[:, offset:offset + length].reshape(batch_rows * length, channels)
        result = result + jnp.dot(window, weight[offset * channels:(offset + 1) * channels], preferred_element_type=jnp.float32)
    return result.reshape(batch_rows, length, weight.shape[1])


def encode(stacked, conv1_w, conv2_w, conv3_w, conv4_w):
    first_layer = jax.nn.gelu(strided_conv(stacked[:, :, None], conv1_w)).astype(jnp.bfloat16)
    second_layer = jax.nn.gelu(strided_conv(first_layer, conv2_w)).astype(jnp.bfloat16)
    third_layer = jax.nn.gelu(centred_conv(second_layer, conv3_w)).astype(jnp.bfloat16)
    return (second_layer.astype(jnp.float32) + centred_conv(third_layer, conv4_w)).astype(jnp.bfloat16)


def stack_rows(gathered, counts):
    running = jnp.zeros((gathered.shape[0], gathered.shape[2]), jnp.float32)
    for slot_index in range(gathered.shape[1]):
        live_mask = (slot_index < counts)[:, None]
        running = running + jnp.where(live_mask, gathered[:, slot_index].astype(jnp.float32), jnp.float32(0.0))
    return (running / counts.astype(jnp.float32)[:, None]).astype(jnp.bfloat16)


def lateral_mix(block_values, weight):
    field_values = block_values.astype(jnp.float32)
    rows_out = field_values.shape[-2]
    cols_out = field_values.shape[-1]
    widths = [(0, 0)] * (field_values.ndim - 2) + [(1, 1), (1, 1)]
    padded = jnp.pad(field_values, widths)
    mixed_sum = field_values
    for row_shift in range(3):
        for col_shift in range(3):
            tap_weight = weight[:, row_shift * 3 + col_shift][:, None, None]
            mixed_sum = mixed_sum + tap_weight * padded[..., row_shift:row_shift + rows_out, col_shift:col_shift + cols_out]
    return mixed_sum.astype(jnp.bfloat16)


def reference(traces, fold_ids, fold_counts, conv1_w, conv2_w, conv3_w, conv4_w, lateral_w):
    block_bins = BI * BX
    ids_blocks = fold_ids.reshape(NIL * NXL // block_bins, block_bins, FOLD)
    counts = fold_counts.reshape(NIL * NXL // block_bins, block_bins)

    def one_block(pieces):
        ids_here, counts_here = pieces
        gathered = jnp.take(traces, ids_here, axis=0)
        return encode(stack_rows(gathered, counts_here), conv1_w, conv2_w, conv3_w, conv4_w)

    features = lax.map(one_block, (ids_blocks, counts))
    volume = features.reshape(NIL, NXL, T2, C2).transpose(2, 3, 0, 1)

    def one_plane(time_plane):
        return lateral_mix(time_plane, lateral_w)

    return lax.map(one_plane, volume)
```

```python
import functools

import jax
import jax.numpy as jnp
import numpy as np
from jax import lax
from jax.experimental import pallas as pl
from jax.experimental.pallas import tpu as pltpu
from jax.sharding import PartitionSpec as P


def stack_rows(gathered, counts):
    running = jnp.zeros((gathered.shape[0], gathered.shape[2]), jnp.float32)
    for slot_index in range(gathered.shape[1]):
        live_mask = (slot_index < counts)[:, None]
        running = running + jnp.where(
            live_mask, gathered[:, slot_index].astype(jnp.float32), jnp.float32(0.0)
        )
    return (running / counts.astype(jnp.float32)[:, None]).astype(jnp.bfloat16)


def lateral_mix(block_values, weight):
    field_values = block_values.astype(jnp.float32)
    rows_out = field_values.shape[-2]
    cols_out = field_values.shape[-1]
    widths = [(0, 0)] * (field_values.ndim - 2) + [(1, 1), (1, 1)]
    padded = jnp.pad(field_values, widths)
    mixed_sum = field_values
    for row_shift in range(3):
        for col_shift in range(3):
            tap_weight = weight[:, row_shift * 3 + col_shift][:, None, None]
            mixed_sum = (
                mixed_sum
                + tap_weight
                * padded[..., row_shift : row_shift + rows_out, col_shift : col_shift + cols_out]
            )
    return mixed_sum.astype(jnp.bfloat16)


def banded_first_weights(conv1_w):
    m_index = jnp.arange(32, dtype=jnp.int32)[:, None, None]
    u_index = jnp.arange(4, dtype=jnp.int32)[None, :, None]
    tap_index = jnp.arange(8, dtype=jnp.int32)[None, None, :]
    selector = (m_index - 4 * u_index - 12 == tap_index).astype(jnp.float32)
    return (
        jnp.einsum("muj,jc->muc", selector, conv1_w.astype(jnp.float32))
        .astype(jnp.bfloat16)
        .reshape(32, 4 * conv1_w.shape[1])
    )


def encoder_kernel(n_il, n_xl, bins, paired_ref, a1_ref, w2_ref, w3_ref, w4_ref, out_ref,
                   first_pad, second_pad, third_pad):
    rows = paired_ref.shape[0]
    width = w2_ref.shape[1]
    chunk = 8 * bins
    n_chunks = rows // chunk
    pair_rows = 2 * bins
    group = width // n_xl
    pairs_per_slab = out_ref.shape[2]
    f32 = jnp.float32

    zeros_pad = jnp.zeros((bins, width), jnp.bfloat16)
    first_pad[pl.ds(0, bins), :] = zeros_pad
    second_pad[pl.ds(0, bins), :] = zeros_pad
    second_pad[pl.ds(bins + rows, bins), :] = zeros_pad
    third_pad[pl.ds(0, bins), :] = zeros_pad
    third_pad[pl.ds(bins + rows, bins), :] = zeros_pad

    def gelu(x):
        return jax.nn.gelu(x)

    def layer1(ci, carry):
        r0 = pl.multiple_of(ci * chunk, chunk)
        x = paired_ref[pl.ds(r0, chunk), :]
        y = jnp.dot(x, a1_ref[...], preferred_element_type=f32)
        first_pad[pl.ds(bins + r0, chunk), :] = gelu(y).astype(jnp.bfloat16)
        return carry

    lax.fori_loop(0, n_chunks, layer1, 0)

    def layer2(ci, carry):
        r0 = pl.multiple_of(ci * chunk, chunk)
        earlier = first_pad[pl.ds(r0, chunk), :]
        current = first_pad[pl.ds(r0 + bins, chunk), :]
        y = jnp.dot(earlier, w2_ref[pl.ds(0, width), :], preferred_element_type=f32)
        y = y + jnp.dot(current, w2_ref[pl.ds(width, width), :], preferred_element_type=f32)
        second_pad[pl.ds(bins + r0, chunk), :] = gelu(y).astype(jnp.bfloat16)
        return carry

    lax.fori_loop(0, n_chunks, layer2, 0)

    def centred(src, w_ref, r0):
        y = jnp.dot(src[pl.ds(r0, chunk), :], w_ref[pl.ds(0, width), :], preferred_element_type=f32)
        y = y + jnp.dot(src[pl.ds(r0 + bins, chunk), :], w_ref[pl.ds(width, width), :],
                        preferred_element_type=f32)
        y = y + jnp.dot(src[pl.ds(r0 + 2 * bins, chunk), :], w_ref[pl.ds(2 * width, width), :],
                        preferred_element_type=f32)
        return y

    def layer3(ci, carry):
        r0 = pl.multiple_of(ci * chunk, chunk)
        y = centred(second_pad, w3_ref, r0)
        third_pad[pl.ds(bins + r0, chunk), :] = gelu(y).astype(jnp.bfloat16)
        return carry

    lax.fori_loop(0, n_chunks, layer3, 0)

    def layer4(ci, carry):
        r0 = pl.multiple_of(ci * chunk, chunk)
        y = centred(third_pad, w4_ref, r0)
        y = y + second_pad[pl.ds(bins + r0, chunk), :].astype(f32)
        feat = y.astype(jnp.bfloat16).astype(f32)
        for p in range(chunk // pair_rows):
            pair = ci * (chunk // pair_rows) + p
            slab = pair // pairs_per_slab
            within = pair % pairs_per_slab
            block = feat[p * pair_rows:(p + 1) * pair_rows, :].T
            out_ref[slab, :, within, :, :] = block.reshape(n_xl, group, pair_rows).astype(
                jnp.bfloat16)
        return carry

    lax.fori_loop(0, n_chunks, layer4, 0)


def encode_to_send(paired, a1, conv2_w, conv3_w, conv4_w, n_il, n_xl, bins, steps):
    rows = paired.shape[0]
    width = conv2_w.shape[1]
    out_shape = jax.ShapeDtypeStruct(
        (n_il, n_xl, steps // n_il // 2, width // n_xl, 2 * bins), jnp.bfloat16)
    return pl.pallas_call(
        functools.partial(encoder_kernel, n_il, n_xl, bins),
        out_shape=out_shape,
        in_specs=[pl.BlockSpec(memory_space=pltpu.VMEM)] * 5,
        out_specs=pl.BlockSpec(memory_space=pltpu.VMEM),
        scratch_shapes=[
            pltpu.VMEM((bins + rows, width), jnp.bfloat16),
            pltpu.VMEM((2 * bins + rows, width), jnp.bfloat16),
            pltpu.VMEM((2 * bins + rows, width), jnp.bfloat16),
        ],
        compiler_params=pltpu.CompilerParams(vmem_limit_bytes=48 * 1024 * 1024),
    )(paired, a1, conv2_w, conv3_w, conv4_w)


def per_device(traces, fold_ids, fold_counts, conv1_w, conv2_w, conv3_w, conv4_w, lateral_w):
    il_count = lax.axis_size("il")
    xl_count = lax.axis_size("xl")
    devices = il_count * xl_count
    rows_here = traces.shape[0]
    samples = traces.shape[1]
    bins_il, bins_xl, fold_depth = fold_ids.shape
    bin_total = bins_il * bins_xl
    slot_total = bin_total * fold_depth
    capacity = 2 * slot_total // devices
    flat_ids = fold_ids.reshape(slot_total)
    source = flat_ids // rows_here
    local_row = flat_ids % rows_here
    onehot = (source[:, None] == jnp.arange(devices, dtype=jnp.int32)[None, :]).astype(jnp.int32)
    slot_rank = jnp.sum(onehot * jnp.cumsum(onehot, axis=0), axis=1) - 1
    position = source * capacity + slot_rank
    requests = (
        jnp.zeros((devices * capacity,), jnp.int32)
        .at[position]
        .set(local_row)
        .reshape(devices, capacity)
    )
    wanted = lax.all_to_all(requests, ("il", "xl"), split_axis=0, concat_axis=0, tiled=True)
    picked = jnp.take(traces, wanted.reshape(-1), axis=0).reshape(
        wanted.shape[0], wanted.shape[1], samples
    )
    arrived = lax.all_to_all(picked, ("il", "xl"), split_axis=0, concat_axis=0, tiled=True)
    gathered = jnp.take(arrived.reshape(devices * capacity, samples), position, axis=0).reshape(
        bin_total, fold_depth, samples
    )
    stacked = stack_rows(gathered, fold_counts.reshape(bin_total))
    steps = samples // 16
    groups = stacked.reshape(bin_total, steps, 16).transpose(1, 0, 2)
    previous = jnp.pad(groups, ((1, 0), (0, 0), (0, 0)))[:steps]
    paired = jnp.concatenate([previous, groups], axis=2).reshape(steps * bin_total, 32)
    outgoing = encode_to_send(
        paired, banded_first_weights(conv1_w), conv2_w, conv3_w, conv4_w,
        il_count, xl_count, bin_total, steps,
    )
    pairs = outgoing.shape[2]
    group_width = outgoing.shape[3]
    outgoing = outgoing.reshape(devices, pairs, group_width, 2 * bin_total)
    received = lax.all_to_all(outgoing, ("il", "xl"), split_axis=0, concat_axis=0, tiled=True)
    placed = received.reshape(
        il_count, xl_count, pairs, group_width, 2, bins_il, bins_xl
    ).transpose(2, 4, 3, 0, 5, 1, 6)
    return lateral_mix(
        placed.reshape(2 * pairs, group_width, il_count * bins_il, xl_count * bins_xl), lateral_w
    )


def solution(mesh):
    return jax.shard_map(
        per_device,
        mesh=mesh,
        in_specs=(
            P(("il", "xl"), None),
            P("il", "xl", None),
            P("il", "xl"),
            P(),
            P(),
            P(),
            P(),
            P("xl", None),
        ),
        out_specs=P("il", "xl", None, None),
        check_vma=False,
    )
```

```python
import functools

import jax
import jax.numpy as jnp
import numpy as np
from jax import lax
from jax.experimental import pallas as pl
from jax.experimental.pallas import tpu as pltpu
from jax.sharding import PartitionSpec as P


def stack_rows(gathered, counts):
    running = jnp.zeros((gathered.shape[0], gathered.shape[2]), jnp.float32)
    for slot_index in range(gathered.shape[1]):
        live_mask = (slot_index < counts)[:, None]
        running = running + jnp.where(
            live_mask, gathered[:, slot_index].astype(jnp.float32), jnp.float32(0.0)
        )
    return (running / counts.astype(jnp.float32)[:, None]).astype(jnp.bfloat16)


def lateral_mix(block_values, weight):
    field_values = block_values.astype(jnp.float32)
    rows_out = field_values.shape[-2]
    cols_out = field_values.shape[-1]
    widths = [(0, 0)] * (field_values.ndim - 2) + [(1, 1), (1, 1)]
    padded = jnp.pad(field_values, widths)
    mixed_sum = field_values
    for row_shift in range(3):
        for col_shift in range(3):
            tap_weight = weight[:, row_shift * 3 + col_shift][:, None, None]
            mixed_sum = (
                mixed_sum
                + tap_weight
                * padded[..., row_shift : row_shift + rows_out, col_shift : col_shift + cols_out]
            )
    return mixed_sum.astype(jnp.bfloat16)


def banded_first_weights(conv1_w):
    m_index = jnp.arange(32, dtype=jnp.int32)[:, None, None]
    u_index = jnp.arange(4, dtype=jnp.int32)[None, :, None]
    tap_index = jnp.arange(8, dtype=jnp.int32)[None, None, :]
    selector = (m_index - 4 * u_index - 12 == tap_index).astype(jnp.float32)
    return (
        jnp.einsum("muj,jc->muc", selector, conv1_w.astype(jnp.float32))
        .astype(jnp.bfloat16)
        .reshape(32, 4 * conv1_w.shape[1])
    )


def encoder_kernel(n_il, n_xl, bins, paired_ref, a1_ref, w2_ref, w3_ref, w4_ref, out_ref,
                   first_pad, second_pad, third_pad):
    rows = paired_ref.shape[0]
    width = w2_ref.shape[1]
    chunk = 8 * bins
    n_chunks = rows // chunk
    pair_rows = 2 * bins
    group = width // n_xl
    pairs_per_slab = out_ref.shape[2]
    f32 = jnp.float32

    zeros_pad = jnp.zeros((bins, width), jnp.bfloat16)
    first_pad[pl.ds(0, bins), :] = zeros_pad
    second_pad[pl.ds(0, bins), :] = zeros_pad
    second_pad[pl.ds(bins + rows, bins), :] = zeros_pad
    third_pad[pl.ds(0, bins), :] = zeros_pad
    third_pad[pl.ds(bins + rows, bins), :] = zeros_pad

    def gelu(x):
        return jax.nn.gelu(x)

    def layer1(ci, carry):
        r0 = pl.multiple_of(ci * chunk, chunk)
        x = paired_ref[pl.ds(r0, chunk), :]
        y = jnp.dot(x, a1_ref[...], preferred_element_type=f32)
        first_pad[pl.ds(bins + r0, chunk), :] = gelu(y).astype(jnp.bfloat16)
        return carry

    lax.fori_loop(0, n_chunks, layer1, 0)

    def layer2(ci, carry):
        r0 = pl.multiple_of(ci * chunk, chunk)
        earlier = first_pad[pl.ds(r0, chunk), :]
        current = first_pad[pl.ds(r0 + bins, chunk), :]
        y = jnp.dot(earlier, w2_ref[pl.ds(0, width), :], preferred_element_type=f32)
        y = y + jnp.dot(current, w2_ref[pl.ds(width, width), :], preferred_element_type=f32)
        second_pad[pl.ds(bins + r0, chunk), :] = gelu(y).astype(jnp.bfloat16)
        return carry

    lax.fori_loop(0, n_chunks, layer2, 0)

    def centred(src, w_ref, r0):
        y = jnp.dot(src[pl.ds(r0, chunk), :], w_ref[pl.ds(0, width), :], preferred_element_type=f32)
        y = y + jnp.dot(src[pl.ds(r0 + bins, chunk), :], w_ref[pl.ds(width, width), :],
                        preferred_element_type=f32)
        y = y + jnp.dot(src[pl.ds(r0 + 2 * bins, chunk), :], w_ref[pl.ds(2 * width, width), :],
                        preferred_element_type=f32)
        return y

    def layer3(ci, carry):
        r0 = pl.multiple_of(ci * chunk, chunk)
        y = centred(second_pad, w3_ref, r0)
        third_pad[pl.ds(bins + r0, chunk), :] = gelu(y).astype(jnp.bfloat16)
        return carry

    lax.fori_loop(0, n_chunks, layer3, 0)

    def layer4(ci, carry):
        r0 = pl.multiple_of(ci * chunk, chunk)
        y = centred(third_pad, w4_ref, r0)
        y = y + second_pad[pl.ds(bins + r0, chunk), :].astype(f32)
        feat = y.astype(jnp.bfloat16).astype(f32)
        for p in range(chunk // pair_rows):
            pair = ci * (chunk // pair_rows) + p
            slab = pair // pairs_per_slab
            within = pair % pairs_per_slab
            block = feat[p * pair_rows:(p + 1) * pair_rows, :].T
            out_ref[slab, :, within, :, :] = block.reshape(n_xl, group, pair_rows).astype(
                jnp.bfloat16)
        return carry

    lax.fori_loop(0, n_chunks, layer4, 0)


def encode_to_send(paired, a1, conv2_w, conv3_w, conv4_w, n_il, n_xl, bins, steps):
    rows = paired.shape[0]
    width = conv2_w.shape[1]
    out_shape = jax.ShapeDtypeStruct(
        (n_il, n_xl, steps // n_il // 2, width // n_xl, 2 * bins), jnp.bfloat16)
    return pl.pallas_call(
        functools.partial(encoder_kernel, n_il, n_xl, bins),
        out_shape=out_shape,
        in_specs=[pl.BlockSpec(memory_space=pltpu.VMEM)] * 5,
        out_specs=pl.BlockSpec(memory_space=pltpu.VMEM),
        scratch_shapes=[
            pltpu.VMEM((bins + rows, width), jnp.bfloat16),
            pltpu.VMEM((2 * bins + rows, width), jnp.bfloat16),
            pltpu.VMEM((2 * bins + rows, width), jnp.bfloat16),
        ],
        compiler_params=pltpu.CompilerParams(vmem_limit_bytes=48 * 1024 * 1024),
    )(paired, a1, conv2_w, conv3_w, conv4_w)


def merge_selectors(n_xl, lanes):
    width = lanes // n_xl
    kk = jnp.arange(2 * lanes, dtype=jnp.int32)[None, :, None]
    m = jnp.arange(n_xl * lanes, dtype=jnp.int32)[None, None, :]
    bp = jnp.arange(n_xl // 2, dtype=jnp.int32)[:, None, None]
    b = 2 * bp + kk // lanes
    lane = kk % lanes
    target = (lane // width) * lanes + width * b + lane % width
    return (m == target).astype(jnp.bfloat16)


def receive_kernel(recv_ref, sel_ref, lw_ref, out_ref, field):
    n_a, n_b, rows_k_o, lanes = recv_ref.shape
    n_s, n_o, n_p, n_q = out_ref.shape
    n_k = rows_k_o // n_o
    width = n_q // n_b
    n_p4 = n_p // n_a
    f32 = jnp.float32

    def merge(a, carry):
        y = None
        for bp in range(n_b // 2):
            x = jnp.concatenate([recv_ref[a, 2 * bp], recv_ref[a, 2 * bp + 1]], axis=1)
            d = jnp.dot(x, sel_ref[bp], preferred_element_type=f32)
            y = d if y is None else y + d
        for k in range(n_k):
            for s2 in range(2):
                for p4 in range(n_p4):
                    blk = y[k * n_o:(k + 1) * n_o, (s2 * n_p4 + p4) * lanes:(s2 * n_p4 + p4 + 1) * lanes]
                    start = (2 * k + s2) * n_o * n_p + n_p4 * a + p4
                    field[pl.ds(start, n_o, stride=n_p), :] = blk
        return carry

    lax.fori_loop(0, n_a, merge, 0)

    row = lax.broadcasted_iota(jnp.int32, (n_p, n_q), 0)
    col = lax.broadcasted_iota(jnp.int32, (n_p, n_q), 1)
    zero = jnp.zeros((n_p, n_q), f32)

    def mix(plane, carry):
        s = plane // n_o
        o = plane % n_o
        f = field[pl.ds(pl.multiple_of(plane * n_p, n_p), n_p), :]
        shifted_rows = [
            jnp.where(row == 0, zero, pltpu.roll(f, 1, 0)),
            f,
            jnp.where(row == n_p - 1, zero, pltpu.roll(f, n_p - 1, 0)),
        ]
        acc = f
        for r in range(3):
            g = shifted_rows[r]
            taps = [
                jnp.where(col == 0, zero, pltpu.roll(g, 1, 1)),
                g,
                jnp.where(col == n_q - 1, zero, pltpu.roll(g, n_q - 1, 1)),
            ]
            for c in range(3):
                acc = acc + lw_ref[o, 3 * r + c] * taps[c]
        out_ref[s, o] = acc.astype(out_ref.dtype)
        return carry

    lax.fori_loop(0, n_s * n_o, mix, 0)


def receive_mix(received, sel, lw, n_s, n_o, n_p, n_q):
    return pl.pallas_call(
        receive_kernel,
        out_shape=jax.ShapeDtypeStruct((n_s, n_o, n_p, n_q), jnp.bfloat16),
        in_specs=[pl.BlockSpec(memory_space=pltpu.VMEM), pl.BlockSpec(memory_space=pltpu.VMEM),
                  pl.BlockSpec(memory_space=pltpu.SMEM)],
        out_specs=pl.BlockSpec(memory_space=pltpu.VMEM),
        scratch_shapes=[pltpu.VMEM((n_s * n_o * n_p, n_q), jnp.float32)],
        compiler_params=pltpu.CompilerParams(vmem_limit_bytes=48 * 1024 * 1024),
    )(received, sel, lw)


def per_device(traces, fold_ids, fold_counts, conv1_w, conv2_w, conv3_w, conv4_w, lateral_w):
    il_count = lax.axis_size("il")
    xl_count = lax.axis_size("xl")
    devices = il_count * xl_count
    rows_here = traces.shape[0]
    samples = traces.shape[1]
    bins_il, bins_xl, fold_depth = fold_ids.shape
    bin_total = bins_il * bins_xl
    slot_total = bin_total * fold_depth
    capacity = 2 * slot_total // devices
    flat_ids = fold_ids.reshape(slot_total)
    source = flat_ids // rows_here
    local_row = flat_ids % rows_here
    onehot = (source[:, None] == jnp.arange(devices, dtype=jnp.int32)[None, :]).astype(jnp.int32)
    slot_rank = jnp.sum(onehot * jnp.cumsum(onehot, axis=0), axis=1) - 1
    position = source * capacity + slot_rank
    requests = (
        jnp.zeros((devices * capacity,), jnp.int32)
        .at[position]
        .set(local_row)
        .reshape(devices, capacity)
    )
    wanted = lax.all_to_all(requests, ("il", "xl"), split_axis=0, concat_axis=0, tiled=True)
    picked = jnp.take(traces, wanted.reshape(-1), axis=0).reshape(
        wanted.shape[0], wanted.shape[1], samples
    )
    arrived = lax.all_to_all(picked, ("il", "xl"), split_axis=0, concat_axis=0, tiled=True)
    gathered = jnp.take(arrived.reshape(devices * capacity, samples), position, axis=0).reshape(
        bin_total, fold_depth, samples
    )
    stacked = stack_rows(gathered, fold_counts.reshape(bin_total))
    steps = samples // 16
    groups = stacked.reshape(bin_total, steps, 16).transpose(1, 0, 2)
    previous = jnp.pad(groups, ((1, 0), (0, 0), (0, 0)))[:steps]
    paired = jnp.concatenate([previous, groups], axis=2).reshape(steps * bin_total, 32)
    outgoing = encode_to_send(
        paired, banded_first_weights(conv1_w), conv2_w, conv3_w, conv4_w,
        il_count, xl_count, bin_total, steps,
    )
    pairs = outgoing.shape[2]
    group_width = outgoing.shape[3]
    outgoing = outgoing.reshape(devices, pairs, group_width, 2 * bin_total)
    received = lax.all_to_all(outgoing, ("il", "xl"), split_axis=0, concat_axis=0, tiled=True)
    received = received.reshape(il_count, xl_count, pairs * group_width, 2 * bin_total)
    return receive_mix(
        received, merge_selectors(xl_count, 2 * bin_total), lateral_w,
        2 * pairs, group_width, il_count * bins_il, xl_count * bins_xl,
    )


def solution(mesh):
    return jax.shard_map(
        per_device,
        mesh=mesh,
        in_specs=(
            P(("il", "xl"), None),
            P("il", "xl", None),
            P("il", "xl"),
            P(),
            P(),
            P(),
            P(),
            P("xl", None),
        ),
        out_specs=P("il", "xl", None, None),
        check_vma=False,
    )
```

```python
import functools

import jax
import jax.numpy as jnp
import numpy as np
from jax import lax
from jax.experimental import pallas as pl
from jax.experimental.pallas import tpu as pltpu
from jax.sharding import PartitionSpec as P


def stack_rows(gathered, counts):
    running = jnp.zeros((gathered.shape[0], gathered.shape[2]), jnp.float32)
    for slot_index in range(gathered.shape[1]):
        live_mask = (slot_index < counts)[:, None]
        running = running + jnp.where(
            live_mask, gathered[:, slot_index].astype(jnp.float32), jnp.float32(0.0)
        )
    return (running / counts.astype(jnp.float32)[:, None]).astype(jnp.bfloat16)


def banded_first_weights(conv1_w):
    m_index = jnp.arange(32, dtype=jnp.int32)[:, None, None]
    u_index = jnp.arange(4, dtype=jnp.int32)[None, :, None]
    tap_index = jnp.arange(8, dtype=jnp.int32)[None, None, :]
    selector = (m_index - 4 * u_index - 12 == tap_index).astype(jnp.float32)
    return (
        jnp.einsum("muj,jc->muc", selector, conv1_w.astype(jnp.float32))
        .astype(jnp.bfloat16)
        .reshape(32, 4 * conv1_w.shape[1])
    )


MESH = pl.DeviceIdType.MESH


def exchange_kernel(n_il, n_xl, x_ref, y_ref, send_sem, recv_sem):
    n = n_il * n_xl
    me = lax.axis_index("il") * n_xl + lax.axis_index("xl")
    barrier = pltpu.get_barrier_semaphore()

    def greet(k, carry):
        d = lax.rem(me + 1 + k, n)
        pl.semaphore_signal(barrier, inc=1, device_id=(d // n_xl, d % n_xl), device_id_type=MESH)
        return carry

    lax.fori_loop(0, n - 1, greet, 0)
    pl.semaphore_wait(barrier, n - 1)
    pltpu.make_async_copy(x_ref.at[me], y_ref.at[me], recv_sem).start()

    def send(k, carry):
        d = lax.rem(me + 1 + k, n)
        pltpu.make_async_remote_copy(
            src_ref=x_ref.at[d], dst_ref=y_ref.at[me], send_sem=send_sem, recv_sem=recv_sem,
            device_id=(d // n_xl, d % n_xl), device_id_type=MESH,
        ).start()
        return carry

    lax.fori_loop(0, n - 1, send, 0)
    pltpu.make_async_copy(y_ref, y_ref, recv_sem).wait()
    pltpu.make_async_copy(x_ref.at[pl.ds(0, n - 1)], y_ref.at[pl.ds(0, n - 1)], send_sem).wait()


def exchange(x, n_il, n_xl, collective_id):
    return pl.pallas_call(
        functools.partial(exchange_kernel, n_il, n_xl),
        out_shape=jax.ShapeDtypeStruct(x.shape, x.dtype),
        in_specs=[pl.BlockSpec(memory_space=pl.ANY)],
        out_specs=pl.BlockSpec(memory_space=pl.ANY),
        scratch_shapes=[pltpu.SemaphoreType.DMA(()), pltpu.SemaphoreType.DMA(())],
        compiler_params=pltpu.CompilerParams(collective_id=collective_id, has_side_effects=True),
    )(x)

def encoder_kernel(n_il, n_xl, bins, paired_ref, a1_ref, w2_ref, w3_ref, w4_ref, out_ref,
                   first_pad, second_pad, third_pad):
    rows = paired_ref.shape[0]
    width = w2_ref.shape[1]
    chunk = 8 * bins
    n_chunks = rows // chunk
    pair_rows = 2 * bins
    group = width // n_xl
    pairs_per_slab = out_ref.shape[2]
    f32 = jnp.float32

    zeros_pad = jnp.zeros((bins, width), jnp.bfloat16)
    first_pad[pl.ds(0, bins), :] = zeros_pad
    second_pad[pl.ds(0, bins), :] = zeros_pad
    second_pad[pl.ds(bins + rows, bins), :] = zeros_pad
    third_pad[pl.ds(0, bins), :] = zeros_pad
    third_pad[pl.ds(bins + rows, bins), :] = zeros_pad

    def gelu(x):
        return jax.nn.gelu(x)

    def layer1(ci, carry):
        r0 = pl.multiple_of(ci * chunk, chunk)
        x = paired_ref[pl.ds(r0, chunk), :]
        y = jnp.dot(x, a1_ref[...], preferred_element_type=f32)
        first_pad[pl.ds(bins + r0, chunk), :] = gelu(y).astype(jnp.bfloat16)
        return carry

    lax.fori_loop(0, n_chunks, layer1, 0)

    def layer2(ci, carry):
        r0 = pl.multiple_of(ci * chunk, chunk)
        earlier = first_pad[pl.ds(r0, chunk), :]
        current = first_pad[pl.ds(r0 + bins, chunk), :]
        y = jnp.dot(earlier, w2_ref[pl.ds(0, width), :], preferred_element_type=f32)
        y = y + jnp.dot(current, w2_ref[pl.ds(width, width), :], preferred_element_type=f32)
        second_pad[pl.ds(bins + r0, chunk), :] = gelu(y).astype(jnp.bfloat16)
        return carry

    lax.fori_loop(0, n_chunks, layer2, 0)

    def centred(src, w_ref, r0):
        y = jnp.dot(src[pl.ds(r0, chunk), :], w_ref[pl.ds(0, width), :], preferred_element_type=f32)
        y = y + jnp.dot(src[pl.ds(r0 + bins, chunk), :], w_ref[pl.ds(width, width), :],
                        preferred_element_type=f32)
        y = y + jnp.dot(src[pl.ds(r0 + 2 * bins, chunk), :], w_ref[pl.ds(2 * width, width), :],
                        preferred_element_type=f32)
        return y

    def layer3(ci, carry):
        r0 = pl.multiple_of(ci * chunk, chunk)
        y = centred(second_pad, w3_ref, r0)
        third_pad[pl.ds(bins + r0, chunk), :] = gelu(y).astype(jnp.bfloat16)
        return carry

    lax.fori_loop(0, n_chunks, layer3, 0)

    def layer4(ci, carry):
        r0 = pl.multiple_of(ci * chunk, chunk)
        y = centred(third_pad, w4_ref, r0)
        y = y + second_pad[pl.ds(bins + r0, chunk), :].astype(f32)
        feat = y.astype(jnp.bfloat16).astype(f32)
        for p in range(chunk // pair_rows):
            pair = ci * (chunk // pair_rows) + p
            slab = pair // pairs_per_slab
            within = pair % pairs_per_slab
            block = feat[p * pair_rows:(p + 1) * pair_rows, :].T
            out_ref[slab, :, within, :, :] = block.reshape(n_xl, group, pair_rows).astype(
                jnp.bfloat16)
        return carry

    lax.fori_loop(0, n_chunks, layer4, 0)


def encode_to_send(paired, a1, conv2_w, conv3_w, conv4_w, n_il, n_xl, bins, steps):
    rows = paired.shape[0]
    width = conv2_w.shape[1]
    out_shape = jax.ShapeDtypeStruct(
        (n_il, n_xl, steps // n_il // 2, width // n_xl, 2 * bins), jnp.bfloat16)
    return pl.pallas_call(
        functools.partial(encoder_kernel, n_il, n_xl, bins),
        out_shape=out_shape,
        in_specs=[pl.BlockSpec(memory_space=pltpu.VMEM)] * 5,
        out_specs=pl.BlockSpec(memory_space=pltpu.VMEM),
        scratch_shapes=[
            pltpu.VMEM((bins + rows, width), jnp.bfloat16),
            pltpu.VMEM((2 * bins + rows, width), jnp.bfloat16),
            pltpu.VMEM((2 * bins + rows, width), jnp.bfloat16),
        ],
        compiler_params=pltpu.CompilerParams(vmem_limit_bytes=48 * 1024 * 1024),
    )(paired, a1, conv2_w, conv3_w, conv4_w)


def merge_selectors(n_xl, lanes):
    width = lanes // n_xl
    kk = jnp.arange(2 * lanes, dtype=jnp.int32)[None, :, None]
    m = jnp.arange(n_xl * lanes, dtype=jnp.int32)[None, None, :]
    bp = jnp.arange(n_xl // 2, dtype=jnp.int32)[:, None, None]
    b = 2 * bp + kk // lanes
    lane = kk % lanes
    target = (lane // width) * lanes + width * b + lane % width
    return (m == target).astype(jnp.bfloat16)


def receive_kernel(recv_ref, sel_ref, lw_ref, out_ref, field):
    n_a, n_b, rows_k_o, lanes = recv_ref.shape
    n_s, n_o, n_p, n_q = out_ref.shape
    n_k = rows_k_o // n_o
    width = n_q // n_b
    n_p4 = n_p // n_a
    f32 = jnp.float32

    def merge(a, carry):
        y = None
        for bp in range(n_b // 2):
            x = jnp.concatenate([recv_ref[a, 2 * bp], recv_ref[a, 2 * bp + 1]], axis=1)
            d = jnp.dot(x, sel_ref[bp], preferred_element_type=f32)
            y = d if y is None else y + d
        for k in range(n_k):
            for s2 in range(2):
                for p4 in range(n_p4):
                    blk = y[k * n_o:(k + 1) * n_o, (s2 * n_p4 + p4) * lanes:(s2 * n_p4 + p4 + 1) * lanes]
                    start = (2 * k + s2) * n_o * n_p + n_p4 * a + p4
                    field[pl.ds(start, n_o, stride=n_p), :] = blk
        return carry

    lax.fori_loop(0, n_a, merge, 0)

    row = lax.broadcasted_iota(jnp.int32, (n_p, n_q), 0)
    col = lax.broadcasted_iota(jnp.int32, (n_p, n_q), 1)
    zero = jnp.zeros((n_p, n_q), f32)

    def mix(plane, carry):
        s = plane // n_o
        o = plane % n_o
        f = field[pl.ds(pl.multiple_of(plane * n_p, n_p), n_p), :]
        shifted_rows = [
            jnp.where(row == 0, zero, pltpu.roll(f, 1, 0)),
            f,
            jnp.where(row == n_p - 1, zero, pltpu.roll(f, n_p - 1, 0)),
        ]
        acc = f
        for r in range(3):
            g = shifted_rows[r]
            taps = [
                jnp.where(col == 0, zero, pltpu.roll(g, 1, 1)),
                g,
                jnp.where(col == n_q - 1, zero, pltpu.roll(g, n_q - 1, 1)),
            ]
            for c in range(3):
                acc = acc + lw_ref[o, 3 * r + c] * taps[c]
        out_ref[s, o] = acc.astype(out_ref.dtype)
        return carry

    lax.fori_loop(0, n_s * n_o, mix, 0)


def receive_mix(received, sel, lw, n_s, n_o, n_p, n_q):
    return pl.pallas_call(
        receive_kernel,
        out_shape=jax.ShapeDtypeStruct((n_s, n_o, n_p, n_q), jnp.bfloat16),
        in_specs=[pl.BlockSpec(memory_space=pltpu.VMEM), pl.BlockSpec(memory_space=pltpu.VMEM),
                  pl.BlockSpec(memory_space=pltpu.SMEM)],
        out_specs=pl.BlockSpec(memory_space=pltpu.VMEM),
        scratch_shapes=[pltpu.VMEM((n_s * n_o * n_p, n_q), jnp.float32)],
        compiler_params=pltpu.CompilerParams(vmem_limit_bytes=48 * 1024 * 1024),
    )(received, sel, lw)


def per_device(traces, fold_ids, fold_counts, conv1_w, conv2_w, conv3_w, conv4_w, lateral_w):
    il_count = lax.axis_size("il")
    xl_count = lax.axis_size("xl")
    devices = il_count * xl_count
    rows_here = traces.shape[0]
    samples = traces.shape[1]
    bins_il, bins_xl, fold_depth = fold_ids.shape
    bin_total = bins_il * bins_xl
    slot_total = bin_total * fold_depth
    capacity = 2 * slot_total // devices
    flat_ids = fold_ids.reshape(slot_total)
    source = flat_ids // rows_here
    local_row = flat_ids % rows_here
    onehot = (source[:, None] == jnp.arange(devices, dtype=jnp.int32)[None, :]).astype(jnp.int32)
    slot_rank = jnp.sum(onehot * jnp.cumsum(onehot, axis=0), axis=1) - 1
    position = source * capacity + slot_rank
    requests = (
        jnp.zeros((devices * capacity,), jnp.int32)
        .at[position]
        .set(local_row)
        .reshape(devices, capacity)
    )
    wanted = lax.all_to_all(requests, ("il", "xl"), split_axis=0, concat_axis=0, tiled=True)
    picked = jnp.take(traces, wanted.reshape(-1), axis=0).reshape(
        wanted.shape[0], wanted.shape[1], samples
    )
    arrived = lax.all_to_all(picked, ("il", "xl"), split_axis=0, concat_axis=0, tiled=True)
    gathered = jnp.take(arrived.reshape(devices * capacity, samples), position, axis=0).reshape(
        bin_total, fold_depth, samples
    )
    stacked = stack_rows(gathered, fold_counts.reshape(bin_total))
    steps = samples // 16
    groups = stacked.reshape(bin_total, steps, 16).transpose(1, 0, 2)
    previous = jnp.pad(groups, ((1, 0), (0, 0), (0, 0)))[:steps]
    paired = jnp.concatenate([previous, groups], axis=2).reshape(steps * bin_total, 32)
    outgoing = encode_to_send(
        paired, banded_first_weights(conv1_w), conv2_w, conv3_w, conv4_w,
        il_count, xl_count, bin_total, steps,
    )
    pairs = outgoing.shape[2]
    group_width = outgoing.shape[3]
    outgoing = outgoing.reshape(devices, pairs, group_width, 2 * bin_total)
    received = exchange(outgoing, il_count, xl_count, 0)
    received = received.reshape(il_count, xl_count, pairs * group_width, 2 * bin_total)
    return receive_mix(
        received, merge_selectors(xl_count, 2 * bin_total), lateral_w,
        2 * pairs, group_width, il_count * bins_il, xl_count * bins_xl,
    )


def solution(mesh):
    return jax.shard_map(
        per_device,
        mesh=mesh,
        in_specs=(
            P(("il", "xl"), None),
            P("il", "xl", None),
            P("il", "xl"),
            P(),
            P(),
            P(),
            P(),
            P("xl", None),
        ),
        out_specs=P("il", "xl", None, None),
        check_vma=False,
    )
```

```python
import functools

import jax
import jax.numpy as jnp
import numpy as np
from jax import lax
from jax.experimental import pallas as pl
from jax.experimental.pallas import tpu as pltpu
from jax.sharding import PartitionSpec as P


def stack_rows(gathered, counts):
    running = jnp.zeros((gathered.shape[0], gathered.shape[2]), jnp.float32)
    for slot_index in range(gathered.shape[1]):
        live_mask = (slot_index < counts)[:, None]
        running = running + jnp.where(
            live_mask, gathered[:, slot_index].astype(jnp.float32), jnp.float32(0.0)
        )
    return (running / counts.astype(jnp.float32)[:, None]).astype(jnp.bfloat16)


def banded_first_weights(conv1_w):
    m_index = jnp.arange(32, dtype=jnp.int32)[:, None, None]
    u_index = jnp.arange(4, dtype=jnp.int32)[None, :, None]
    tap_index = jnp.arange(8, dtype=jnp.int32)[None, None, :]
    selector = (m_index - 4 * u_index - 12 == tap_index).astype(jnp.float32)
    return (
        jnp.einsum("muj,jc->muc", selector, conv1_w.astype(jnp.float32))
        .astype(jnp.bfloat16)
        .reshape(32, 4 * conv1_w.shape[1])
    )


MESH = pl.DeviceIdType.MESH


def exchange_kernel(n_il, n_xl, x_ref, y_ref, send_sem, recv_sem):
    n = n_il * n_xl
    me = lax.axis_index("il") * n_xl + lax.axis_index("xl")
    barrier = pltpu.get_barrier_semaphore()

    def greet(k, carry):
        d = lax.rem(me + 1 + k, n)
        pl.semaphore_signal(barrier, inc=1, device_id=(d // n_xl, d % n_xl), device_id_type=MESH)
        return carry

    lax.fori_loop(0, n - 1, greet, 0)
    pl.semaphore_wait(barrier, n - 1)
    pltpu.make_async_copy(x_ref.at[me], y_ref.at[me], recv_sem).start()

    def send(k, carry):
        d = lax.rem(me + 1 + k, n)
        pltpu.make_async_remote_copy(
            src_ref=x_ref.at[d], dst_ref=y_ref.at[me], send_sem=send_sem, recv_sem=recv_sem,
            device_id=(d // n_xl, d % n_xl), device_id_type=MESH,
        ).start()
        return carry

    lax.fori_loop(0, n - 1, send, 0)
    pltpu.make_async_copy(y_ref, y_ref, recv_sem).wait()
    pltpu.make_async_copy(x_ref.at[pl.ds(0, n - 1)], y_ref.at[pl.ds(0, n - 1)], send_sem).wait()


def exchange(x, n_il, n_xl, collective_id):
    return pl.pallas_call(
        functools.partial(exchange_kernel, n_il, n_xl),
        out_shape=jax.ShapeDtypeStruct(x.shape, x.dtype),
        in_specs=[pl.BlockSpec(memory_space=pl.ANY)],
        out_specs=pl.BlockSpec(memory_space=pl.ANY),
        scratch_shapes=[pltpu.SemaphoreType.DMA(()), pltpu.SemaphoreType.DMA(())],
        compiler_params=pltpu.CompilerParams(collective_id=collective_id, has_side_effects=True),
    )(x)

def encoder_kernel(n_il, n_xl, bins, paired_ref, a1_ref, w2_ref, w3_ref, w4_ref, out_ref,
                   first_pad, second_pad, third_pad):
    rows = paired_ref.shape[0]
    width = w2_ref.shape[1]
    chunk = 8 * bins
    n_chunks = rows // chunk
    pair_rows = 2 * bins
    group = width // n_xl
    pairs_per_slab = out_ref.shape[2]
    f32 = jnp.float32

    zeros_pad = jnp.zeros((bins, width), jnp.bfloat16)
    first_pad[pl.ds(0, bins), :] = zeros_pad
    second_pad[pl.ds(0, bins), :] = zeros_pad
    second_pad[pl.ds(bins + rows, bins), :] = zeros_pad
    third_pad[pl.ds(0, bins), :] = zeros_pad
    third_pad[pl.ds(bins + rows, bins), :] = zeros_pad

    def gelu(x):
        return jax.nn.gelu(x)

    def layer1(ci, carry):
        r0 = pl.multiple_of(ci * chunk, chunk)
        x = paired_ref[pl.ds(r0, chunk), :]
        y = jnp.dot(x, a1_ref[...], preferred_element_type=f32)
        first_pad[pl.ds(bins + r0, chunk), :] = gelu(y).astype(jnp.bfloat16)
        return carry

    lax.fori_loop(0, n_chunks, layer1, 0)

    def layer2(ci, carry):
        r0 = pl.multiple_of(ci * chunk, chunk)
        earlier = first_pad[pl.ds(r0, chunk), :]
        current = first_pad[pl.ds(r0 + bins, chunk), :]
        y = jnp.dot(earlier, w2_ref[pl.ds(0, width), :], preferred_element_type=f32)
        y = y + jnp.dot(current, w2_ref[pl.ds(width, width), :], preferred_element_type=f32)
        second_pad[pl.ds(bins + r0, chunk), :] = gelu(y).astype(jnp.bfloat16)
        return carry

    lax.fori_loop(0, n_chunks, layer2, 0)

    def centred(src, w_ref, r0):
        y = jnp.dot(src[pl.ds(r0, chunk), :], w_ref[pl.ds(0, width), :], preferred_element_type=f32)
        y = y + jnp.dot(src[pl.ds(r0 + bins, chunk), :], w_ref[pl.ds(width, width), :],
                        preferred_element_type=f32)
        y = y + jnp.dot(src[pl.ds(r0 + 2 * bins, chunk), :], w_ref[pl.ds(2 * width, width), :],
                        preferred_element_type=f32)
        return y

    def layer3(ci, carry):
        r0 = pl.multiple_of(ci * chunk, chunk)
        y = centred(second_pad, w3_ref, r0)
        third_pad[pl.ds(bins + r0, chunk), :] = gelu(y).astype(jnp.bfloat16)
        return carry

    lax.fori_loop(0, n_chunks, layer3, 0)

    def layer4(ci, carry):
        r0 = pl.multiple_of(ci * chunk, chunk)
        y = centred(third_pad, w4_ref, r0)
        y = y + second_pad[pl.ds(bins + r0, chunk), :].astype(f32)
        feat = y.astype(jnp.bfloat16).astype(f32)
        for p in range(chunk // pair_rows):
            pair = ci * (chunk // pair_rows) + p
            slab = pair // pairs_per_slab
            within = pair % pairs_per_slab
            block = feat[p * pair_rows:(p + 1) * pair_rows, :].T
            out_ref[slab, :, within, :, :] = block.reshape(n_xl, group, pair_rows).astype(
                jnp.bfloat16)
        return carry

    lax.fori_loop(0, n_chunks, layer4, 0)


def encode_to_send(paired, a1, conv2_w, conv3_w, conv4_w, n_il, n_xl, bins, steps):
    rows = paired.shape[0]
    width = conv2_w.shape[1]
    out_shape = jax.ShapeDtypeStruct(
        (n_il, n_xl, steps // n_il // 2, width // n_xl, 2 * bins), jnp.bfloat16)
    return pl.pallas_call(
        functools.partial(encoder_kernel, n_il, n_xl, bins),
        out_shape=out_shape,
        in_specs=[pl.BlockSpec(memory_space=pltpu.VMEM)] * 5,
        out_specs=pl.BlockSpec(memory_space=pltpu.VMEM),
        scratch_shapes=[
            pltpu.VMEM((bins + rows, width), jnp.bfloat16),
            pltpu.VMEM((2 * bins + rows, width), jnp.bfloat16),
            pltpu.VMEM((2 * bins + rows, width), jnp.bfloat16),
        ],
        compiler_params=pltpu.CompilerParams(vmem_limit_bytes=48 * 1024 * 1024),
    )(paired, a1, conv2_w, conv3_w, conv4_w)


def merge_selectors(n_xl, lanes):
    width = lanes // n_xl
    kk = jnp.arange(2 * lanes, dtype=jnp.int32)[None, :, None]
    m = jnp.arange(n_xl * lanes, dtype=jnp.int32)[None, None, :]
    bp = jnp.arange(n_xl // 2, dtype=jnp.int32)[:, None, None]
    b = 2 * bp + kk // lanes
    lane = kk % lanes
    target = (lane // width) * lanes + width * b + lane % width
    return (m == target).astype(jnp.bfloat16)


def lane_tap_matrices(weight, lanes):
    offset = jnp.arange(lanes)[:, None] - jnp.arange(lanes)[None, :] + 1
    taps = weight.reshape(weight.shape[0], 3, 3)
    picked = jnp.where(
        (offset >= 0) & (offset <= 2),
        jnp.take(taps, jnp.clip(offset, 0, 2), axis=2),
        jnp.float32(0.0),
    )
    high = picked.astype(jnp.bfloat16)
    low = (picked - high.astype(jnp.float32)).astype(jnp.bfloat16)
    return jnp.stack([high, low], axis=2)


def receive_kernel(recv_ref, sel_ref, taps_ref, out_ref, field):
    n_a, n_b, rows_k_o, lanes = recv_ref.shape
    n_s, n_o, n_p, n_q = out_ref.shape
    n_k = rows_k_o // n_o
    n_p4 = n_p // n_a
    per_o = n_s * n_p
    f32 = jnp.float32

    def merge(a, carry):
        y = None
        for bp in range(n_b // 2):
            x = jnp.concatenate([recv_ref[a, 2 * bp], recv_ref[a, 2 * bp + 1]], axis=1)
            d = jnp.dot(x, sel_ref[bp], preferred_element_type=f32)
            y = d if y is None else y + d
        for k in range(n_k):
            for s2 in range(2):
                for p4 in range(n_p4):
                    blk = y[k * n_o:(k + 1) * n_o, (s2 * n_p4 + p4) * lanes:(s2 * n_p4 + p4 + 1) * lanes]
                    start = (2 * k + s2) * n_p + n_p4 * a + p4
                    field[pl.ds(start, n_o, stride=per_o), :] = blk
        return carry

    lax.fori_loop(0, n_a, merge, 0)

    row = lax.broadcasted_iota(jnp.int32, (per_o, n_q), 0) % n_p
    zero = jnp.zeros((per_o, n_q), f32)

    def mix(o, carry):
        f = field[pl.ds(pl.multiple_of(o * per_o, per_o), per_o), :]
        fb = f.astype(jnp.bfloat16)
        g = []
        for r in range(3):
            t = jnp.dot(fb, taps_ref[o, r, 0], preferred_element_type=f32)
            t = t + jnp.dot(fb, taps_ref[o, r, 1], preferred_element_type=f32)
            g.append(t)
        acc = f + g[1]
        acc = acc + jnp.where(row == 0, zero, pltpu.roll(g[0], 1, 0))
        acc = acc + jnp.where(row == n_p - 1, zero, pltpu.roll(g[2], per_o - 1, 0))
        out_ref[:, o] = acc.astype(out_ref.dtype).reshape(n_s, n_p, n_q)
        return carry

    lax.fori_loop(0, n_o, mix, 0)


def receive_mix(received, sel, lw, n_s, n_o, n_p, n_q):
    return pl.pallas_call(
        receive_kernel,
        out_shape=jax.ShapeDtypeStruct((n_s, n_o, n_p, n_q), jnp.bfloat16),
        in_specs=[pl.BlockSpec(memory_space=pltpu.VMEM)] * 3,
        out_specs=pl.BlockSpec(memory_space=pltpu.VMEM),
        scratch_shapes=[pltpu.VMEM((n_s * n_o * n_p, n_q), jnp.float32)],
        compiler_params=pltpu.CompilerParams(vmem_limit_bytes=48 * 1024 * 1024),
    )(received, sel, lw)


def per_device(traces, fold_ids, fold_counts, conv1_w, conv2_w, conv3_w, conv4_w, lateral_w):
    il_count = lax.axis_size("il")
    xl_count = lax.axis_size("xl")
    devices = il_count * xl_count
    rows_here = traces.shape[0]
    samples = traces.shape[1]
    bins_il, bins_xl, fold_depth = fold_ids.shape
    bin_total = bins_il * bins_xl
    slot_total = bin_total * fold_depth
    capacity = 2 * slot_total // devices
    flat_ids = fold_ids.reshape(slot_total)
    source = flat_ids // rows_here
    local_row = flat_ids % rows_here
    onehot = (source[:, None] == jnp.arange(devices, dtype=jnp.int32)[None, :]).astype(jnp.int32)
    slot_rank = jnp.sum(onehot * jnp.cumsum(onehot, axis=0), axis=1) - 1
    position = source * capacity + slot_rank
    requests = (
        jnp.zeros((devices * capacity,), jnp.int32)
        .at[position]
        .set(local_row)
        .reshape(devices, capacity)
    )
    wanted = lax.all_to_all(requests, ("il", "xl"), split_axis=0, concat_axis=0, tiled=True)
    picked = jnp.take(traces, wanted.reshape(-1), axis=0).reshape(
        wanted.shape[0], wanted.shape[1], samples
    )
    arrived = lax.all_to_all(picked, ("il", "xl"), split_axis=0, concat_axis=0, tiled=True)
    gathered = jnp.take(arrived.reshape(devices * capacity, samples), position, axis=0).reshape(
        bin_total, fold_depth, samples
    )
    stacked = stack_rows(gathered, fold_counts.reshape(bin_total))
    steps = samples // 16
    groups = stacked.reshape(bin_total, steps, 16).transpose(1, 0, 2)
    previous = jnp.pad(groups, ((1, 0), (0, 0), (0, 0)))[:steps]
    paired = jnp.concatenate([previous, groups], axis=2).reshape(steps * bin_total, 32)
    outgoing = encode_to_send(
        paired, banded_first_weights(conv1_w), conv2_w, conv3_w, conv4_w,
        il_count, xl_count, bin_total, steps,
    )
    pairs = outgoing.shape[2]
    group_width = outgoing.shape[3]
    outgoing = outgoing.reshape(devices, pairs, group_width, 2 * bin_total)
    received = lax.all_to_all(outgoing, ("il", "xl"), split_axis=0, concat_axis=0, tiled=True)
    received = received.reshape(il_count, xl_count, pairs * group_width, 2 * bin_total)
    return receive_mix(
        received, merge_selectors(xl_count, 2 * bin_total),
        lane_tap_matrices(lateral_w, xl_count * bins_xl),
        2 * pairs, group_width, il_count * bins_il, xl_count * bins_xl,
    )


def solution(mesh):
    return jax.shard_map(
        per_device,
        mesh=mesh,
        in_specs=(
            P(("il", "xl"), None),
            P("il", "xl", None),
            P("il", "xl"),
            P(),
            P(),
            P(),
            P(),
            P("xl", None),
        ),
        out_specs=P("il", "xl", None, None),
        check_vma=False,
    )
```

```python
import functools

import jax
import jax.numpy as jnp
import numpy as np
from jax import lax
from jax.experimental import pallas as pl
from jax.experimental.pallas import tpu as pltpu
from jax.sharding import PartitionSpec as P


def stack_rows(gathered, counts):
    running = jnp.zeros((gathered.shape[0], gathered.shape[2]), jnp.float32)
    for slot_index in range(gathered.shape[1]):
        live_mask = (slot_index < counts)[:, None]
        running = running + jnp.where(
            live_mask, gathered[:, slot_index].astype(jnp.float32), jnp.float32(0.0)
        )
    return (running / counts.astype(jnp.float32)[:, None]).astype(jnp.bfloat16)


def banded_first_weights(conv1_w):
    m_index = jnp.arange(32, dtype=jnp.int32)[:, None, None]
    u_index = jnp.arange(4, dtype=jnp.int32)[None, :, None]
    tap_index = jnp.arange(8, dtype=jnp.int32)[None, None, :]
    selector = (m_index - 4 * u_index - 12 == tap_index).astype(jnp.float32)
    return (
        jnp.einsum("muj,jc->muc", selector, conv1_w.astype(jnp.float32))
        .astype(jnp.bfloat16)
        .reshape(32, 4 * conv1_w.shape[1])
    )


MESH = pl.DeviceIdType.MESH


def exchange_kernel(n_il, n_xl, x_ref, y_ref, send_sem, recv_sem):
    n = n_il * n_xl
    me = lax.axis_index("il") * n_xl + lax.axis_index("xl")
    barrier = pltpu.get_barrier_semaphore()

    def greet(k, carry):
        d = lax.rem(me + 1 + k, n)
        pl.semaphore_signal(barrier, inc=1, device_id=(d // n_xl, d % n_xl), device_id_type=MESH)
        return carry

    lax.fori_loop(0, n - 1, greet, 0)
    pl.semaphore_wait(barrier, n - 1)
    pltpu.make_async_copy(x_ref.at[me], y_ref.at[me], recv_sem).start()

    def send(k, carry):
        d = lax.rem(me + 1 + k, n)
        pltpu.make_async_remote_copy(
            src_ref=x_ref.at[d], dst_ref=y_ref.at[me], send_sem=send_sem, recv_sem=recv_sem,
            device_id=(d // n_xl, d % n_xl), device_id_type=MESH,
        ).start()
        return carry

    lax.fori_loop(0, n - 1, send, 0)
    pltpu.make_async_copy(y_ref, y_ref, recv_sem).wait()
    pltpu.make_async_copy(x_ref.at[pl.ds(0, n - 1)], y_ref.at[pl.ds(0, n - 1)], send_sem).wait()


def exchange(x, n_il, n_xl, collective_id):
    return pl.pallas_call(
        functools.partial(exchange_kernel, n_il, n_xl),
        out_shape=jax.ShapeDtypeStruct(x.shape, x.dtype),
        in_specs=[pl.BlockSpec(memory_space=pl.ANY)],
        out_specs=pl.BlockSpec(memory_space=pl.ANY),
        scratch_shapes=[pltpu.SemaphoreType.DMA(()), pltpu.SemaphoreType.DMA(())],
        compiler_params=pltpu.CompilerParams(collective_id=collective_id, has_side_effects=True),
    )(x)

def encoder_kernel(n_il, n_xl, bins, paired_ref, a1_ref, w2_ref, w3_ref, w4_ref, out_ref,
                   first_pad, second_pad, third_pad):
    rows = paired_ref.shape[0]
    width = w2_ref.shape[1]
    chunk = 8 * bins
    n_chunks = rows // chunk
    pair_rows = 2 * bins
    group = width // n_xl
    pairs_per_slab = out_ref.shape[2]
    f32 = jnp.float32

    zeros_pad = jnp.zeros((bins, width), jnp.bfloat16)
    first_pad[pl.ds(0, bins), :] = zeros_pad
    second_pad[pl.ds(0, bins), :] = zeros_pad
    second_pad[pl.ds(bins + rows, bins), :] = zeros_pad
    third_pad[pl.ds(0, bins), :] = zeros_pad
    third_pad[pl.ds(bins + rows, bins), :] = zeros_pad

    def gelu(x):
        return jax.nn.gelu(x)

    def layer1(ci, carry):
        r0 = pl.multiple_of(ci * chunk, chunk)
        x = paired_ref[pl.ds(r0, chunk), :]
        y = jnp.dot(x, a1_ref[...], preferred_element_type=f32)
        first_pad[pl.ds(bins + r0, chunk), :] = gelu(y).astype(jnp.bfloat16)
        return carry

    lax.fori_loop(0, n_chunks, layer1, 0)

    def layer2(ci, carry):
        r0 = pl.multiple_of(ci * chunk, chunk)
        earlier = first_pad[pl.ds(r0, chunk), :]
        current = first_pad[pl.ds(r0 + bins, chunk), :]
        y = jnp.dot(earlier, w2_ref[pl.ds(0, width), :], preferred_element_type=f32)
        y = y + jnp.dot(current, w2_ref[pl.ds(width, width), :], preferred_element_type=f32)
        second_pad[pl.ds(bins + r0, chunk), :] = gelu(y).astype(jnp.bfloat16)
        return carry

    lax.fori_loop(0, n_chunks, layer2, 0)

    def centred(src, w_ref, r0):
        y = jnp.dot(src[pl.ds(r0, chunk), :], w_ref[pl.ds(0, width), :], preferred_element_type=f32)
        y = y + jnp.dot(src[pl.ds(r0 + bins, chunk), :], w_ref[pl.ds(width, width), :],
                        preferred_element_type=f32)
        y = y + jnp.dot(src[pl.ds(r0 + 2 * bins, chunk), :], w_ref[pl.ds(2 * width, width), :],
                        preferred_element_type=f32)
        return y

    def layer3(ci, carry):
        r0 = pl.multiple_of(ci * chunk, chunk)
        y = centred(second_pad, w3_ref, r0)
        third_pad[pl.ds(bins + r0, chunk), :] = gelu(y).astype(jnp.bfloat16)
        return carry

    lax.fori_loop(0, n_chunks, layer3, 0)

    def layer4(ci, carry):
        r0 = pl.multiple_of(ci * chunk, chunk)
        y = centred(third_pad, w4_ref, r0)
        y = y + second_pad[pl.ds(bins + r0, chunk), :].astype(f32)
        feat = y.astype(jnp.bfloat16).astype(f32)
        for p in range(chunk // pair_rows):
            pair = ci * (chunk // pair_rows) + p
            slab = pair // pairs_per_slab
            within = pair % pairs_per_slab
            block = feat[p * pair_rows:(p + 1) * pair_rows, :].T
            out_ref[slab, :, within, :, :] = block.reshape(n_xl, group, pair_rows).astype(
                jnp.bfloat16)
        return carry

    lax.fori_loop(0, n_chunks, layer4, 0)


def encode_to_send(paired, a1, conv2_w, conv3_w, conv4_w, n_il, n_xl, bins, steps):
    rows = paired.shape[0]
    width = conv2_w.shape[1]
    out_shape = jax.ShapeDtypeStruct(
        (n_il, n_xl, steps // n_il // 2, width // n_xl, 2 * bins), jnp.bfloat16)
    return pl.pallas_call(
        functools.partial(encoder_kernel, n_il, n_xl, bins),
        out_shape=out_shape,
        in_specs=[pl.BlockSpec(memory_space=pltpu.VMEM)] * 5,
        out_specs=pl.BlockSpec(memory_space=pltpu.VMEM),
        scratch_shapes=[
            pltpu.VMEM((bins + rows, width), jnp.bfloat16),
            pltpu.VMEM((2 * bins + rows, width), jnp.bfloat16),
            pltpu.VMEM((2 * bins + rows, width), jnp.bfloat16),
        ],
        compiler_params=pltpu.CompilerParams(vmem_limit_bytes=48 * 1024 * 1024),
    )(paired, a1, conv2_w, conv3_w, conv4_w)


def merge_selectors(n_xl, lanes):
    width = lanes // n_xl
    kk = jnp.arange(2 * lanes, dtype=jnp.int32)[None, :, None]
    m = jnp.arange(n_xl * lanes, dtype=jnp.int32)[None, None, :]
    bp = jnp.arange(n_xl // 2, dtype=jnp.int32)[:, None, None]
    b = 2 * bp + kk // lanes
    lane = kk % lanes
    target = (lane // width) * lanes + width * b + lane % width
    return (m == target).astype(jnp.bfloat16)


def lane_tap_matrices(weight, lanes):
    offset = jnp.arange(lanes)[:, None] - jnp.arange(lanes)[None, :] + 1
    taps = weight.reshape(weight.shape[0], 3, 3, 1, 1)
    picked = jnp.zeros((weight.shape[0], 3, lanes, lanes), jnp.float32)
    for c in range(3):
        picked = picked + jnp.where(offset == c, taps[:, :, c], jnp.float32(0.0))
    high = lax.reduce_precision(picked, exponent_bits=8, mantissa_bits=7)
    low = (picked - high).astype(jnp.bfloat16)
    return jnp.stack([high.astype(jnp.bfloat16), low], axis=2)


def receive_kernel(recv_ref, sel_ref, taps_ref, out_ref, field):
    n_a, n_b, rows_k_o, lanes = recv_ref.shape
    n_s, n_o, n_p, n_q = out_ref.shape
    n_k = rows_k_o // n_o
    n_p4 = n_p // n_a
    per_o = n_s * n_p
    f32 = jnp.float32

    def merge(a, carry):
        y = None
        for bp in range(n_b // 2):
            x = jnp.concatenate([recv_ref[a, 2 * bp], recv_ref[a, 2 * bp + 1]], axis=1)
            d = jnp.dot(x, sel_ref[bp], preferred_element_type=f32)
            y = d if y is None else y + d
        for k in range(n_k):
            for s2 in range(2):
                for p4 in range(n_p4):
                    blk = y[k * n_o:(k + 1) * n_o, (s2 * n_p4 + p4) * lanes:(s2 * n_p4 + p4 + 1) * lanes]
                    start = (2 * k + s2) * n_p + n_p4 * a + p4
                    field[pl.ds(start, n_o, stride=per_o), :] = blk
        return carry

    lax.fori_loop(0, n_a, merge, 0)

    row = lax.broadcasted_iota(jnp.int32, (per_o, n_q), 0) % n_p
    zero = jnp.zeros((per_o, n_q), f32)

    def mix(o, carry):
        f = field[pl.ds(pl.multiple_of(o * per_o, per_o), per_o), :]
        fb = f.astype(jnp.bfloat16)
        g = []
        for r in range(3):
            t = jnp.dot(fb, taps_ref[o, r, 0], preferred_element_type=f32)
            t = t + jnp.dot(fb, taps_ref[o, r, 1], preferred_element_type=f32)
            g.append(t)
        acc = f + g[1]
        acc = acc + jnp.where(row == 0, zero, pltpu.roll(g[0], 1, 0))
        acc = acc + jnp.where(row == n_p - 1, zero, pltpu.roll(g[2], per_o - 1, 0))
        out_ref[:, o] = acc.astype(out_ref.dtype).reshape(n_s, n_p, n_q)
        return carry

    lax.fori_loop(0, n_o, mix, 0)


def receive_mix(received, sel, lw, n_s, n_o, n_p, n_q):
    return pl.pallas_call(
        receive_kernel,
        out_shape=jax.ShapeDtypeStruct((n_s, n_o, n_p, n_q), jnp.bfloat16),
        in_specs=[pl.BlockSpec(memory_space=pltpu.VMEM)] * 3,
        out_specs=pl.BlockSpec(memory_space=pltpu.VMEM),
        scratch_shapes=[pltpu.VMEM((n_s * n_o * n_p, n_q), jnp.float32)],
        compiler_params=pltpu.CompilerParams(vmem_limit_bytes=48 * 1024 * 1024),
    )(received, sel, lw)


def per_device(traces, fold_ids, fold_counts, conv1_w, conv2_w, conv3_w, conv4_w, lateral_w):
    il_count = lax.axis_size("il")
    xl_count = lax.axis_size("xl")
    devices = il_count * xl_count
    rows_here = traces.shape[0]
    samples = traces.shape[1]
    bins_il, bins_xl, fold_depth = fold_ids.shape
    bin_total = bins_il * bins_xl
    slot_total = bin_total * fold_depth
    capacity = 2 * slot_total // devices
    flat_ids = fold_ids.reshape(slot_total)
    source = flat_ids // rows_here
    local_row = flat_ids % rows_here
    onehot = (source[:, None] == jnp.arange(devices, dtype=jnp.int32)[None, :]).astype(jnp.int32)
    slot_rank = jnp.sum(onehot * jnp.cumsum(onehot, axis=0), axis=1) - 1
    position = source * capacity + slot_rank
    requests = (
        jnp.zeros((devices * capacity,), jnp.int32)
        .at[position]
        .set(local_row)
        .reshape(devices, capacity)
    )
    wanted = lax.all_to_all(requests, ("il", "xl"), split_axis=0, concat_axis=0, tiled=True)
    picked = jnp.take(traces, wanted.reshape(-1), axis=0).reshape(
        wanted.shape[0], wanted.shape[1], samples
    )
    arrived = lax.all_to_all(picked, ("il", "xl"), split_axis=0, concat_axis=0, tiled=True)
    gathered = jnp.take(arrived.reshape(devices * capacity, samples), position, axis=0).reshape(
        bin_total, fold_depth, samples
    )
    stacked = stack_rows(gathered, fold_counts.reshape(bin_total))
    steps = samples // 16
    groups = stacked.reshape(bin_total, steps, 16).transpose(1, 0, 2)
    previous = jnp.pad(groups, ((1, 0), (0, 0), (0, 0)))[:steps]
    paired = jnp.concatenate([previous, groups], axis=2).reshape(steps * bin_total, 32)
    outgoing = encode_to_send(
        paired, banded_first_weights(conv1_w), conv2_w, conv3_w, conv4_w,
        il_count, xl_count, bin_total, steps,
    )
    pairs = outgoing.shape[2]
    group_width = outgoing.shape[3]
    outgoing = outgoing.reshape(devices, pairs, group_width, 2 * bin_total)
    received = lax.all_to_all(outgoing, ("il", "xl"), split_axis=0, concat_axis=0, tiled=True)
    received = received.reshape(il_count, xl_count, pairs * group_width, 2 * bin_total)
    return receive_mix(
        received, merge_selectors(xl_count, 2 * bin_total),
        lane_tap_matrices(lateral_w, xl_count * bins_xl),
        2 * pairs, group_width, il_count * bins_il, xl_count * bins_xl,
    )


def solution(mesh):
    return jax.shard_map(
        per_device,
        mesh=mesh,
        in_specs=(
            P(("il", "xl"), None),
            P("il", "xl", None),
            P("il", "xl"),
            P(),
            P(),
            P(),
            P(),
            P("xl", None),
        ),
        out_specs=P("il", "xl", None, None),
        check_vma=False,
    )
```

```python
import functools

import jax
import jax.numpy as jnp
import numpy as np
from jax import lax
from jax.experimental import pallas as pl
from jax.experimental.pallas import tpu as pltpu
from jax.sharding import PartitionSpec as P


def stack_rows(gathered, counts):
    running = jnp.zeros((gathered.shape[0], gathered.shape[2]), jnp.float32)
    for slot_index in range(gathered.shape[1]):
        live_mask = (slot_index < counts)[:, None]
        running = running + jnp.where(
            live_mask, gathered[:, slot_index].astype(jnp.float32), jnp.float32(0.0)
        )
    return (running / counts.astype(jnp.float32)[:, None]).astype(jnp.bfloat16)


def banded_first_weights(conv1_w):
    m_index = jnp.arange(32, dtype=jnp.int32)[:, None, None]
    u_index = jnp.arange(4, dtype=jnp.int32)[None, :, None]
    tap_index = jnp.arange(8, dtype=jnp.int32)[None, None, :]
    selector = (m_index - 4 * u_index - 12 == tap_index).astype(jnp.float32)
    return (
        jnp.einsum("muj,jc->muc", selector, conv1_w.astype(jnp.float32))
        .astype(jnp.bfloat16)
        .reshape(32, 4 * conv1_w.shape[1])
    )


MESH = pl.DeviceIdType.MESH


def exchange_kernel(n_il, n_xl, x_ref, y_ref, send_sem, recv_sem):
    n = n_il * n_xl
    me = lax.axis_index("il") * n_xl + lax.axis_index("xl")
    barrier = pltpu.get_barrier_semaphore()

    def greet(k, carry):
        d = lax.rem(me + 1 + k, n)
        pl.semaphore_signal(barrier, inc=1, device_id=(d // n_xl, d % n_xl), device_id_type=MESH)
        return carry

    lax.fori_loop(0, n - 1, greet, 0)
    pl.semaphore_wait(barrier, n - 1)
    pltpu.make_async_copy(x_ref.at[me], y_ref.at[me], recv_sem).start()

    def send(k, carry):
        d = lax.rem(me + 1 + k, n)
        pltpu.make_async_remote_copy(
            src_ref=x_ref.at[d], dst_ref=y_ref.at[me], send_sem=send_sem, recv_sem=recv_sem,
            device_id=(d // n_xl, d % n_xl), device_id_type=MESH,
        ).start()
        return carry

    lax.fori_loop(0, n - 1, send, 0)
    pltpu.make_async_copy(y_ref, y_ref, recv_sem).wait()
    pltpu.make_async_copy(x_ref.at[pl.ds(0, n - 1)], y_ref.at[pl.ds(0, n - 1)], send_sem).wait()


def exchange(x, n_il, n_xl, collective_id):
    return pl.pallas_call(
        functools.partial(exchange_kernel, n_il, n_xl),
        out_shape=jax.ShapeDtypeStruct(x.shape, x.dtype),
        in_specs=[pl.BlockSpec(memory_space=pl.ANY)],
        out_specs=pl.BlockSpec(memory_space=pl.ANY),
        scratch_shapes=[pltpu.SemaphoreType.DMA(()), pltpu.SemaphoreType.DMA(())],
        compiler_params=pltpu.CompilerParams(collective_id=collective_id, has_side_effects=True),
    )(x)

def encoder_kernel(n_il, n_xl, bins, paired_ref, a1_ref, w2_ref, w3_ref, w4_ref, out_ref,
                   first_pad, second_pad, third_pad):
    rows = paired_ref.shape[0]
    width = w2_ref.shape[1]
    chunk = 8 * bins
    n_chunks = rows // chunk
    pair_rows = 2 * bins
    group = width // n_xl
    pairs_per_slab = out_ref.shape[2]
    f32 = jnp.float32

    zeros_pad = jnp.zeros((bins, width), jnp.bfloat16)
    first_pad[pl.ds(0, bins), :] = zeros_pad
    second_pad[pl.ds(0, bins), :] = zeros_pad
    second_pad[pl.ds(bins + rows, bins), :] = zeros_pad
    third_pad[pl.ds(0, bins), :] = zeros_pad
    third_pad[pl.ds(bins + rows, bins), :] = zeros_pad

    def gelu(x):
        return jax.nn.gelu(x)

    def layer1(ci, carry):
        r0 = pl.multiple_of(ci * chunk, chunk)
        x = paired_ref[pl.ds(r0, chunk), :]
        y = jnp.dot(x, a1_ref[...], preferred_element_type=f32)
        first_pad[pl.ds(bins + r0, chunk), :] = gelu(y).astype(jnp.bfloat16)
        return carry

    lax.fori_loop(0, n_chunks, layer1, 0)

    def layer2(ci, carry):
        r0 = pl.multiple_of(ci * chunk, chunk)
        earlier = first_pad[pl.ds(r0, chunk), :]
        current = first_pad[pl.ds(r0 + bins, chunk), :]
        y = jnp.dot(earlier, w2_ref[pl.ds(0, width), :], preferred_element_type=f32)
        y = y + jnp.dot(current, w2_ref[pl.ds(width, width), :], preferred_element_type=f32)
        second_pad[pl.ds(bins + r0, chunk), :] = gelu(y).astype(jnp.bfloat16)
        return carry

    lax.fori_loop(0, n_chunks, layer2, 0)

    def centred(src, w_ref, r0):
        y = jnp.dot(src[pl.ds(r0, chunk), :], w_ref[pl.ds(0, width), :], preferred_element_type=f32)
        y = y + jnp.dot(src[pl.ds(r0 + bins, chunk), :], w_ref[pl.ds(width, width), :],
                        preferred_element_type=f32)
        y = y + jnp.dot(src[pl.ds(r0 + 2 * bins, chunk), :], w_ref[pl.ds(2 * width, width), :],
                        preferred_element_type=f32)
        return y

    def layer3(ci, carry):
        r0 = pl.multiple_of(ci * chunk, chunk)
        y = centred(second_pad, w3_ref, r0)
        third_pad[pl.ds(bins + r0, chunk), :] = gelu(y).astype(jnp.bfloat16)
        return carry

    lax.fori_loop(0, n_chunks, layer3, 0)

    def layer4(ci, carry):
        r0 = pl.multiple_of(ci * chunk, chunk)
        y = centred(third_pad, w4_ref, r0)
        y = y + second_pad[pl.ds(bins + r0, chunk), :].astype(f32)
        feat = y.astype(jnp.bfloat16).astype(f32)
        for p in range(chunk // pair_rows):
            pair = ci * (chunk // pair_rows) + p
            slab = pair // pairs_per_slab
            within = pair % pairs_per_slab
            block = feat[p * pair_rows:(p + 1) * pair_rows, :].T
            out_ref[slab, :, within, :, :] = block.reshape(n_xl, group, pair_rows).astype(
                jnp.bfloat16)
        return carry

    lax.fori_loop(0, n_chunks, layer4, 0)


def encode_to_send(paired, a1, conv2_w, conv3_w, conv4_w, n_il, n_xl, bins, steps):
    rows = paired.shape[0]
    width = conv2_w.shape[1]
    out_shape = jax.ShapeDtypeStruct(
        (n_il, n_xl, steps // n_il // 2, width // n_xl, 2 * bins), jnp.bfloat16)
    return pl.pallas_call(
        functools.partial(encoder_kernel, n_il, n_xl, bins),
        out_shape=out_shape,
        in_specs=[pl.BlockSpec(memory_space=pltpu.VMEM)] * 5,
        out_specs=pl.BlockSpec(memory_space=pltpu.VMEM),
        scratch_shapes=[
            pltpu.VMEM((bins + rows, width), jnp.bfloat16),
            pltpu.VMEM((2 * bins + rows, width), jnp.bfloat16),
            pltpu.VMEM((2 * bins + rows, width), jnp.bfloat16),
        ],
        compiler_params=pltpu.CompilerParams(vmem_limit_bytes=48 * 1024 * 1024),
    )(paired, a1, conv2_w, conv3_w, conv4_w)


def merge_selectors(n_xl, lanes):
    width = lanes // n_xl
    kk = jnp.arange(2 * lanes, dtype=jnp.int32)[None, :, None]
    m = jnp.arange(n_xl * lanes, dtype=jnp.int32)[None, None, :]
    bp = jnp.arange(n_xl // 2, dtype=jnp.int32)[:, None, None]
    b = 2 * bp + kk // lanes
    lane = kk % lanes
    target = (lane // width) * lanes + width * b + lane % width
    return (m == target).astype(jnp.bfloat16)


def lane_tap_matrices(weight, lanes):
    offset = jnp.arange(lanes)[:, None] - jnp.arange(lanes)[None, :] + 1
    taps = weight.reshape(weight.shape[0], 3, 3, 1, 1)
    picked = jnp.zeros((weight.shape[0], 3, lanes, lanes), jnp.float32)
    for c in range(3):
        picked = picked + jnp.where(offset == c, taps[:, :, c], jnp.float32(0.0))
    high = lax.reduce_precision(picked, exponent_bits=8, mantissa_bits=7)
    low = (picked - high).astype(jnp.bfloat16)
    return jnp.stack([high.astype(jnp.bfloat16), low], axis=2)


def receive_kernel(recv_ref, sel_ref, taps_ref, out_ref, field):
    n_a, n_b, rows_k_o, lanes = recv_ref.shape
    n_s, n_o, n_p, n_q = out_ref.shape
    n_k = rows_k_o // n_o
    n_p4 = n_p // n_a
    per_o = n_s * n_p
    f32 = jnp.float32

    def merge(a, carry):
        y = None
        for bp in range(n_b // 2):
            x = jnp.concatenate([recv_ref[a, 2 * bp], recv_ref[a, 2 * bp + 1]], axis=1)
            d = jnp.dot(x, sel_ref[bp], preferred_element_type=f32)
            y = d if y is None else y + d
        for k in range(n_k):
            for s2 in range(2):
                for p4 in range(n_p4):
                    blk = y[k * n_o:(k + 1) * n_o, (s2 * n_p4 + p4) * lanes:(s2 * n_p4 + p4 + 1) * lanes]
                    start = (2 * k + s2) * n_p + n_p4 * a + p4
                    field[pl.ds(start, n_o, stride=per_o), :] = blk
        return carry

    lax.fori_loop(0, n_a, merge, 0)

    row = lax.broadcasted_iota(jnp.int32, (per_o, n_q), 0) % n_p
    zero = jnp.zeros((per_o, n_q), f32)

    def mix(o, carry):
        f = field[pl.ds(pl.multiple_of(o * per_o, per_o), per_o), :]
        fb = f.astype(jnp.bfloat16)
        g = []
        for r in range(3):
            t = jnp.dot(fb, taps_ref[o, r, 0], preferred_element_type=f32)
            t = t + jnp.dot(fb, taps_ref[o, r, 1], preferred_element_type=f32)
            g.append(t)
        acc = f + g[1]
        acc = acc + jnp.where(row == 0, zero, pltpu.roll(g[0], 1, 0))
        acc = acc + jnp.where(row == n_p - 1, zero, pltpu.roll(g[2], per_o - 1, 0))
        out_ref[:, o] = acc.astype(out_ref.dtype).reshape(n_s, n_p, n_q)
        return carry

    lax.fori_loop(0, n_o, mix, 0)


def receive_mix(received, sel, lw, n_s, n_o, n_p, n_q):
    return pl.pallas_call(
        receive_kernel,
        out_shape=jax.ShapeDtypeStruct((n_s, n_o, n_p, n_q), jnp.bfloat16),
        in_specs=[pl.BlockSpec(memory_space=pltpu.VMEM)] * 3,
        out_specs=pl.BlockSpec(memory_space=pltpu.VMEM),
        scratch_shapes=[pltpu.VMEM((n_s * n_o * n_p, n_q), jnp.float32)],
        compiler_params=pltpu.CompilerParams(vmem_limit_bytes=48 * 1024 * 1024),
    )(received, sel, lw)


def per_device(traces, fold_ids, fold_counts, conv1_w, conv2_w, conv3_w, conv4_w, lateral_w):
    il_count = lax.axis_size("il")
    xl_count = lax.axis_size("xl")
    devices = il_count * xl_count
    rows_here = traces.shape[0]
    samples = traces.shape[1]
    bins_il, bins_xl, fold_depth = fold_ids.shape
    bin_total = bins_il * bins_xl
    slot_total = bin_total * fold_depth
    capacity = 2 * slot_total // devices
    flat_ids = fold_ids.reshape(slot_total)
    source = flat_ids // rows_here
    local_row = flat_ids % rows_here
    onehot = (source[:, None] == jnp.arange(devices, dtype=jnp.int32)[None, :]).astype(jnp.int32)
    slot_rank = jnp.sum(onehot * jnp.cumsum(onehot, axis=0), axis=1) - 1
    position = source * capacity + slot_rank
    requests = (
        jnp.zeros((devices * capacity,), jnp.int32)
        .at[position]
        .set(local_row)
        .reshape(devices, capacity)
    )
    wanted = exchange(requests, il_count, xl_count, 1)
    picked = jnp.take(traces, wanted.reshape(-1), axis=0).reshape(
        wanted.shape[0], wanted.shape[1], samples
    )
    arrived = lax.all_to_all(picked, ("il", "xl"), split_axis=0, concat_axis=0, tiled=True)
    gathered = jnp.take(arrived.reshape(devices * capacity, samples), position, axis=0).reshape(
        bin_total, fold_depth, samples
    )
    stacked = stack_rows(gathered, fold_counts.reshape(bin_total))
    steps = samples // 16
    groups = stacked.reshape(bin_total, steps, 16).transpose(1, 0, 2)
    previous = jnp.pad(groups, ((1, 0), (0, 0), (0, 0)))[:steps]
    paired = jnp.concatenate([previous, groups], axis=2).reshape(steps * bin_total, 32)
    outgoing = encode_to_send(
        paired, banded_first_weights(conv1_w), conv2_w, conv3_w, conv4_w,
        il_count, xl_count, bin_total, steps,
    )
    pairs = outgoing.shape[2]
    group_width = outgoing.shape[3]
    outgoing = outgoing.reshape(devices, pairs, group_width, 2 * bin_total)
    received = lax.all_to_all(outgoing, ("il", "xl"), split_axis=0, concat_axis=0, tiled=True)
    received = received.reshape(il_count, xl_count, pairs * group_width, 2 * bin_total)
    return receive_mix(
        received, merge_selectors(xl_count, 2 * bin_total),
        lane_tap_matrices(lateral_w, xl_count * bins_xl),
        2 * pairs, group_width, il_count * bins_il, xl_count * bins_xl,
    )


def solution(mesh):
    return jax.shard_map(
        per_device,
        mesh=mesh,
        in_specs=(
            P(("il", "xl"), None),
            P("il", "xl", None),
            P("il", "xl"),
            P(),
            P(),
            P(),
            P(),
            P("xl", None),
        ),
        out_specs=P("il", "xl", None, None),
        check_vma=False,
    )
```

```python
import functools

import jax
import jax.numpy as jnp
import numpy as np
from jax import lax
from jax.experimental import pallas as pl
from jax.experimental.pallas import tpu as pltpu
from jax.sharding import PartitionSpec as P


def window_first_weights(conv1_w, window):
    l_index = jnp.arange(window, dtype=jnp.int32)[None, :, None, None]
    c_index = jnp.arange(9, dtype=jnp.int32)[:, None, None, None]
    u_index = jnp.arange(4, dtype=jnp.int32)[None, None, :, None]
    tap_index = jnp.arange(8, dtype=jnp.int32)[None, None, None, :]
    start = jnp.where(c_index < 8, 16 * c_index + 12, -4)
    selector = (l_index - start - 4 * u_index == tap_index).astype(jnp.float32)
    return (
        jnp.einsum("clut,to->cluo", selector, conv1_w.astype(jnp.float32))
        .astype(jnp.bfloat16)
        .reshape(9, window, 4 * conv1_w.shape[1])
    )


MESH = pl.DeviceIdType.MESH


def exchange_kernel(n_il, n_xl, x_ref, y_ref, send_sem, recv_sem):
    n = n_il * n_xl
    me = lax.axis_index("il") * n_xl + lax.axis_index("xl")
    barrier = pltpu.get_barrier_semaphore()

    def greet(k, carry):
        d = lax.rem(me + 1 + k, n)
        pl.semaphore_signal(barrier, inc=1, device_id=(d // n_xl, d % n_xl), device_id_type=MESH)
        return carry

    lax.fori_loop(0, n - 1, greet, 0)
    pl.semaphore_wait(barrier, n - 1)
    pltpu.make_async_copy(x_ref.at[me], y_ref.at[me], recv_sem).start()

    def send(k, carry):
        d = lax.rem(me + 1 + k, n)
        pltpu.make_async_remote_copy(
            src_ref=x_ref.at[d], dst_ref=y_ref.at[me], send_sem=send_sem, recv_sem=recv_sem,
            device_id=(d // n_xl, d % n_xl), device_id_type=MESH,
        ).start()
        return carry

    lax.fori_loop(0, n - 1, send, 0)
    pltpu.make_async_copy(y_ref, y_ref, recv_sem).wait()
    pltpu.make_async_copy(x_ref.at[pl.ds(0, n - 1)], y_ref.at[pl.ds(0, n - 1)], send_sem).wait()


def exchange(x, n_il, n_xl, collective_id):
    return pl.pallas_call(
        functools.partial(exchange_kernel, n_il, n_xl),
        out_shape=jax.ShapeDtypeStruct(x.shape, x.dtype),
        in_specs=[pl.BlockSpec(memory_space=pl.ANY)],
        out_specs=pl.BlockSpec(memory_space=pl.ANY),
        scratch_shapes=[pltpu.SemaphoreType.DMA(()), pltpu.SemaphoreType.DMA(())],
        compiler_params=pltpu.CompilerParams(collective_id=collective_id, has_side_effects=True),
    )(x)

def encoder_kernel(n_il, n_xl, bins, gathered_ref, counts_ref, b1_ref, w2_ref, w3_ref, w4_ref,
                   out_ref, stacked, paired, first_pad, second_pad, third_pad):
    fold, _, samples = gathered_ref.shape
    width = w2_ref.shape[1]
    rows = first_pad.shape[0] - bins
    chunk = 8 * bins
    n_chunks = rows // chunk
    pair_rows = 2 * bins
    group = width // n_xl
    pairs_per_slab = out_ref.shape[2]
    blocks = samples // 128
    f32 = jnp.float32

    zeros_pad = jnp.zeros((bins, width), jnp.bfloat16)
    first_pad[pl.ds(0, bins), :] = zeros_pad
    second_pad[pl.ds(0, bins), :] = zeros_pad
    second_pad[pl.ds(bins + rows, bins), :] = zeros_pad
    third_pad[pl.ds(0, bins), :] = zeros_pad
    third_pad[pl.ds(bins + rows, bins), :] = zeros_pad

    counts = counts_ref[...]
    running = jnp.zeros((bins, samples), f32)
    for slot in range(fold):
        running = running + jnp.where(slot < counts, gathered_ref[slot].astype(f32), f32(0.0))
    stacked[:, pl.ds(0, samples)] = (running / counts.astype(f32)).astype(jnp.bfloat16)
    stacked[:, pl.ds(samples, 128)] = jnp.zeros((bins, 128), jnp.bfloat16)
    for m in range(blocks):
        paired[pl.ds(m * bins, bins), :] = stacked[:, pl.ds(m * 128, 256)]

    def gelu(x):
        return jax.nn.gelu(x)

    def layer1(c, carry):
        y = jnp.dot(paired[...], b1_ref[c], preferred_element_type=f32)
        y = gelu(y).astype(jnp.bfloat16)
        for m in range(blocks):
            step = 1 + c + 8 * m
            if m == blocks - 1:
                @pl.when(c < 7)
                def _():
                    first_pad[pl.ds(pl.multiple_of(bins + bins * step, bins), bins), :] = (
                        y[m * bins:(m + 1) * bins])
            else:
                first_pad[pl.ds(pl.multiple_of(bins + bins * step, bins), bins), :] = (
                    y[m * bins:(m + 1) * bins])
        return carry

    lax.fori_loop(0, 8, layer1, 0)
    y0 = jnp.dot(paired[pl.ds(0, bins), :], b1_ref[8], preferred_element_type=f32)
    first_pad[pl.ds(bins, bins), :] = gelu(y0).astype(jnp.bfloat16)

    def layer2(ci, carry):
        r0 = pl.multiple_of(ci * chunk, chunk)
        earlier = first_pad[pl.ds(r0, chunk), :]
        current = first_pad[pl.ds(r0 + bins, chunk), :]
        y = jnp.dot(earlier, w2_ref[pl.ds(0, width), :], preferred_element_type=f32)
        y = y + jnp.dot(current, w2_ref[pl.ds(width, width), :], preferred_element_type=f32)
        second_pad[pl.ds(bins + r0, chunk), :] = gelu(y).astype(jnp.bfloat16)
        return carry

    lax.fori_loop(0, n_chunks, layer2, 0)

    def centred(src, w_ref, r0):
        y = jnp.dot(src[pl.ds(r0, chunk), :], w_ref[pl.ds(0, width), :], preferred_element_type=f32)
        y = y + jnp.dot(src[pl.ds(r0 + bins, chunk), :], w_ref[pl.ds(width, width), :],
                        preferred_element_type=f32)
        y = y + jnp.dot(src[pl.ds(r0 + 2 * bins, chunk), :], w_ref[pl.ds(2 * width, width), :],
                        preferred_element_type=f32)
        return y

    def layer3(ci, carry):
        r0 = pl.multiple_of(ci * chunk, chunk)
        y = centred(second_pad, w3_ref, r0)
        third_pad[pl.ds(bins + r0, chunk), :] = gelu(y).astype(jnp.bfloat16)
        return carry

    lax.fori_loop(0, n_chunks, layer3, 0)

    def layer4(ci, carry):
        r0 = pl.multiple_of(ci * chunk, chunk)
        y = centred(third_pad, w4_ref, r0)
        y = y + second_pad[pl.ds(bins + r0, chunk), :].astype(f32)
        feat = y.astype(jnp.bfloat16).astype(f32)
        for p in range(chunk // pair_rows):
            pair = ci * (chunk // pair_rows) + p
            slab = pair // pairs_per_slab
            within = pair % pairs_per_slab
            block = feat[p * pair_rows:(p + 1) * pair_rows, :].T
            out_ref[slab, :, within, :, :] = block.reshape(n_xl, group, pair_rows).astype(
                jnp.bfloat16)
        return carry

    lax.fori_loop(0, n_chunks, layer4, 0)


def encode_to_send(gathered, counts, b1, conv2_w, conv3_w, conv4_w, n_il, n_xl):
    fold, bins, samples = gathered.shape
    steps = samples // 16
    rows = steps * bins
    width = conv2_w.shape[1]
    out_shape = jax.ShapeDtypeStruct(
        (n_il, n_xl, steps // n_il // 2, width // n_xl, 2 * bins), jnp.bfloat16)
    return pl.pallas_call(
        functools.partial(encoder_kernel, n_il, n_xl, bins),
        out_shape=out_shape,
        in_specs=[pl.BlockSpec(memory_space=pltpu.VMEM)] * 6,
        out_specs=pl.BlockSpec(memory_space=pltpu.VMEM),
        scratch_shapes=[
            pltpu.VMEM((bins, samples + 128), jnp.bfloat16),
            pltpu.VMEM((samples // 128 * bins, 256), jnp.bfloat16),
            pltpu.VMEM((bins + rows, width), jnp.bfloat16),
            pltpu.VMEM((2 * bins + rows, width), jnp.bfloat16),
            pltpu.VMEM((2 * bins + rows, width), jnp.bfloat16),
        ],
        compiler_params=pltpu.CompilerParams(vmem_limit_bytes=48 * 1024 * 1024),
    )(gathered, counts, b1, conv2_w, conv3_w, conv4_w)


def merge_selectors(n_xl, lanes):
    width = lanes // n_xl
    kk = jnp.arange(2 * lanes, dtype=jnp.int32)[None, :, None]
    m = jnp.arange(n_xl * lanes, dtype=jnp.int32)[None, None, :]
    bp = jnp.arange(n_xl // 2, dtype=jnp.int32)[:, None, None]
    b = 2 * bp + kk // lanes
    lane = kk % lanes
    target = (lane // width) * lanes + width * b + lane % width
    return (m == target).astype(jnp.bfloat16)


def lane_tap_matrices(weight, lanes):
    offset = jnp.arange(lanes)[:, None] - jnp.arange(lanes)[None, :] + 1
    taps = weight.reshape(weight.shape[0], 3, 3, 1, 1)
    picked = jnp.zeros((weight.shape[0], 3, lanes, lanes), jnp.float32)
    for c in range(3):
        picked = picked + jnp.where(offset == c, taps[:, :, c], jnp.float32(0.0))
    high = lax.reduce_precision(picked, exponent_bits=8, mantissa_bits=7)
    low = (picked - high).astype(jnp.bfloat16)
    return jnp.stack([high.astype(jnp.bfloat16), low], axis=2)


def receive_kernel(recv_ref, sel_ref, taps_ref, out_ref, field):
    n_a, n_b, rows_k_o, lanes = recv_ref.shape
    n_s, n_o, n_p, n_q = out_ref.shape
    n_k = rows_k_o // n_o
    n_p4 = n_p // n_a
    per_o = n_s * n_p
    f32 = jnp.float32

    def merge(a, carry):
        y = None
        for bp in range(n_b // 2):
            x = jnp.concatenate([recv_ref[a, 2 * bp], recv_ref[a, 2 * bp + 1]], axis=1)
            d = jnp.dot(x, sel_ref[bp], preferred_element_type=f32)
            y = d if y is None else y + d
        for k in range(n_k):
            for s2 in range(2):
                for p4 in range(n_p4):
                    blk = y[k * n_o:(k + 1) * n_o, (s2 * n_p4 + p4) * lanes:(s2 * n_p4 + p4 + 1) * lanes]
                    start = (2 * k + s2) * n_p + n_p4 * a + p4
                    field[pl.ds(start, n_o, stride=per_o), :] = blk
        return carry

    lax.fori_loop(0, n_a, merge, 0)

    row = lax.broadcasted_iota(jnp.int32, (per_o, n_q), 0) % n_p
    zero = jnp.zeros((per_o, n_q), f32)

    def mix(o, carry):
        f = field[pl.ds(pl.multiple_of(o * per_o, per_o), per_o), :]
        fb = f.astype(jnp.bfloat16)
        g = []
        for r in range(3):
            t = jnp.dot(fb, taps_ref[o, r, 0], preferred_element_type=f32)
            t = t + jnp.dot(fb, taps_ref[o, r, 1], preferred_element_type=f32)
            g.append(t)
        acc = f + g[1]
        acc = acc + jnp.where(row == 0, zero, pltpu.roll(g[0], 1, 0))
        acc = acc + jnp.where(row == n_p - 1, zero, pltpu.roll(g[2], per_o - 1, 0))
        out_ref[:, o] = acc.astype(out_ref.dtype).reshape(n_s, n_p, n_q)
        return carry

    lax.fori_loop(0, n_o, mix, 0)


def receive_mix(received, sel, lw, n_s, n_o, n_p, n_q):
    return pl.pallas_call(
        receive_kernel,
        out_shape=jax.ShapeDtypeStruct((n_s, n_o, n_p, n_q), jnp.bfloat16),
        in_specs=[pl.BlockSpec(memory_space=pltpu.VMEM)] * 3,
        out_specs=pl.BlockSpec(memory_space=pltpu.VMEM),
        scratch_shapes=[pltpu.VMEM((n_s * n_o * n_p, n_q), jnp.float32)],
        compiler_params=pltpu.CompilerParams(vmem_limit_bytes=48 * 1024 * 1024),
    )(received, sel, lw)


def per_device(traces, fold_ids, fold_counts, conv1_w, conv2_w, conv3_w, conv4_w, lateral_w):
    il_count = lax.axis_size("il")
    xl_count = lax.axis_size("xl")
    devices = il_count * xl_count
    rows_here = traces.shape[0]
    samples = traces.shape[1]
    bins_il, bins_xl, fold_depth = fold_ids.shape
    bin_total = bins_il * bins_xl
    slot_total = bin_total * fold_depth
    capacity = 2 * slot_total // devices
    flat_ids = fold_ids.reshape(slot_total)
    source = flat_ids // rows_here
    local_row = flat_ids % rows_here
    onehot = (source[:, None] == jnp.arange(devices, dtype=jnp.int32)[None, :]).astype(jnp.int32)
    slot_rank = jnp.sum(onehot * jnp.cumsum(onehot, axis=0), axis=1) - 1
    position = source * capacity + slot_rank
    requests = (
        jnp.zeros((devices * capacity,), jnp.int32)
        .at[position]
        .set(local_row)
        .reshape(devices, capacity)
    )
    wanted = exchange(requests, il_count, xl_count, 1)
    picked = jnp.take(traces, wanted.reshape(-1), axis=0).reshape(
        wanted.shape[0], wanted.shape[1], samples
    )
    arrived = lax.all_to_all(picked, ("il", "xl"), split_axis=0, concat_axis=0, tiled=True)
    slot_major = position.reshape(bin_total, fold_depth).T.reshape(slot_total)
    gathered = jnp.take(arrived.reshape(devices * capacity, samples), slot_major, axis=0).reshape(
        fold_depth, bin_total, samples
    )
    outgoing = encode_to_send(
        gathered, fold_counts.reshape(bin_total, 1), window_first_weights(conv1_w, 256),
        conv2_w, conv3_w, conv4_w, il_count, xl_count,
    )
    pairs = outgoing.shape[2]
    group_width = outgoing.shape[3]
    outgoing = outgoing.reshape(devices, pairs, group_width, 2 * bin_total)
    received = lax.all_to_all(outgoing, ("il", "xl"), split_axis=0, concat_axis=0, tiled=True)
    received = received.reshape(il_count, xl_count, pairs * group_width, 2 * bin_total)
    return receive_mix(
        received, merge_selectors(xl_count, 2 * bin_total),
        lane_tap_matrices(lateral_w, xl_count * bins_xl),
        2 * pairs, group_width, il_count * bins_il, xl_count * bins_xl,
    )


def solution(mesh):
    return jax.shard_map(
        per_device,
        mesh=mesh,
        in_specs=(
            P(("il", "xl"), None),
            P("il", "xl", None),
            P("il", "xl"),
            P(),
            P(),
            P(),
            P(),
            P("xl", None),
        ),
        out_specs=P("il", "xl", None, None),
        check_vma=False,
    )
```

```python
import functools

import jax
import jax.numpy as jnp
import numpy as np
from jax import lax
from jax.experimental import pallas as pl
from jax.experimental.pallas import tpu as pltpu
from jax.sharding import PartitionSpec as P


def window_first_weights(conv1_w, window):
    l_index = jnp.arange(window, dtype=jnp.int32)[None, :, None, None]
    c_index = jnp.arange(9, dtype=jnp.int32)[:, None, None, None]
    u_index = jnp.arange(4, dtype=jnp.int32)[None, None, :, None]
    tap_index = jnp.arange(8, dtype=jnp.int32)[None, None, None, :]
    start = jnp.where(c_index < 8, 16 * c_index + 12, -4)
    selector = (l_index - start - 4 * u_index == tap_index).astype(jnp.float32)
    return (
        jnp.einsum("clut,to->cluo", selector, conv1_w.astype(jnp.float32))
        .astype(jnp.bfloat16)
        .reshape(9, window, 4 * conv1_w.shape[1])
    )


MESH = pl.DeviceIdType.MESH


def exchange_kernel(n_il, n_xl, x_ref, y_ref, send_sem, recv_sem):
    n = n_il * n_xl
    me = lax.axis_index("il") * n_xl + lax.axis_index("xl")
    barrier = pltpu.get_barrier_semaphore()

    def greet(k, carry):
        d = lax.rem(me + 1 + k, n)
        pl.semaphore_signal(barrier, inc=1, device_id=(d // n_xl, d % n_xl), device_id_type=MESH)
        return carry

    lax.fori_loop(0, n - 1, greet, 0)
    pl.semaphore_wait(barrier, n - 1)
    pltpu.make_async_copy(x_ref.at[me], y_ref.at[me], recv_sem).start()

    def send(k, carry):
        d = lax.rem(me + 1 + k, n)
        pltpu.make_async_remote_copy(
            src_ref=x_ref.at[d], dst_ref=y_ref.at[me], send_sem=send_sem, recv_sem=recv_sem,
            device_id=(d // n_xl, d % n_xl), device_id_type=MESH,
        ).start()
        return carry

    lax.fori_loop(0, n - 1, send, 0)
    pltpu.make_async_copy(y_ref, y_ref, recv_sem).wait()
    pltpu.make_async_copy(x_ref.at[pl.ds(0, n - 1)], y_ref.at[pl.ds(0, n - 1)], send_sem).wait()


def exchange(x, n_il, n_xl, collective_id):
    return pl.pallas_call(
        functools.partial(exchange_kernel, n_il, n_xl),
        out_shape=jax.ShapeDtypeStruct(x.shape, x.dtype),
        in_specs=[pl.BlockSpec(memory_space=pl.ANY)],
        out_specs=pl.BlockSpec(memory_space=pl.ANY),
        scratch_shapes=[pltpu.SemaphoreType.DMA(()), pltpu.SemaphoreType.DMA(())],
        compiler_params=pltpu.CompilerParams(collective_id=collective_id, has_side_effects=True),
    )(x)

def encoder_kernel(n_il, n_xl, bins, arrived_ref, select_ref, counts_ref, b1_ref, w2_ref, w3_ref,
                   w4_ref, out_ref, stacked, paired, first_pad, second_pad, third_pad):
    samples = arrived_ref.shape[1]
    width = w2_ref.shape[1]
    rows = first_pad.shape[0] - bins
    chunk = 8 * bins
    n_chunks = rows // chunk
    pair_rows = 2 * bins
    group = width // n_xl
    pairs_per_slab = out_ref.shape[2]
    blocks = samples // 128
    f32 = jnp.float32

    zeros_pad = jnp.zeros((bins, width), jnp.bfloat16)
    first_pad[pl.ds(0, bins), :] = zeros_pad
    second_pad[pl.ds(0, bins), :] = zeros_pad
    second_pad[pl.ds(bins + rows, bins), :] = zeros_pad
    third_pad[pl.ds(0, bins), :] = zeros_pad
    third_pad[pl.ds(bins + rows, bins), :] = zeros_pad

    counts = counts_ref[...]
    running = jnp.dot(select_ref[...], arrived_ref[...], preferred_element_type=f32)
    stacked[:, pl.ds(0, samples)] = (running / counts.astype(f32)).astype(jnp.bfloat16)
    stacked[:, pl.ds(samples, 128)] = jnp.zeros((bins, 128), jnp.bfloat16)
    for m in range(blocks):
        paired[pl.ds(m * bins, bins), :] = stacked[:, pl.ds(m * 128, 256)]

    def gelu(x):
        return jax.nn.gelu(x)

    def layer1(c, carry):
        y = jnp.dot(paired[...], b1_ref[c], preferred_element_type=f32)
        y = gelu(y).astype(jnp.bfloat16)
        for m in range(blocks):
            step = 1 + c + 8 * m
            if m == blocks - 1:
                @pl.when(c < 7)
                def _():
                    first_pad[pl.ds(pl.multiple_of(bins + bins * step, bins), bins), :] = (
                        y[m * bins:(m + 1) * bins])
            else:
                first_pad[pl.ds(pl.multiple_of(bins + bins * step, bins), bins), :] = (
                    y[m * bins:(m + 1) * bins])
        return carry

    lax.fori_loop(0, 8, layer1, 0)
    y0 = jnp.dot(paired[pl.ds(0, bins), :], b1_ref[8], preferred_element_type=f32)
    first_pad[pl.ds(bins, bins), :] = gelu(y0).astype(jnp.bfloat16)

    def layer2(ci, carry):
        r0 = pl.multiple_of(ci * chunk, chunk)
        earlier = first_pad[pl.ds(r0, chunk), :]
        current = first_pad[pl.ds(r0 + bins, chunk), :]
        y = jnp.dot(earlier, w2_ref[pl.ds(0, width), :], preferred_element_type=f32)
        y = y + jnp.dot(current, w2_ref[pl.ds(width, width), :], preferred_element_type=f32)
        second_pad[pl.ds(bins + r0, chunk), :] = gelu(y).astype(jnp.bfloat16)
        return carry

    lax.fori_loop(0, n_chunks, layer2, 0)

    def centred(src, w_ref, r0):
        y = jnp.dot(src[pl.ds(r0, chunk), :], w_ref[pl.ds(0, width), :], preferred_element_type=f32)
        y = y + jnp.dot(src[pl.ds(r0 + bins, chunk), :], w_ref[pl.ds(width, width), :],
                        preferred_element_type=f32)
        y = y + jnp.dot(src[pl.ds(r0 + 2 * bins, chunk), :], w_ref[pl.ds(2 * width, width), :],
                        preferred_element_type=f32)
        return y

    def layer3(ci, carry):
        r0 = pl.multiple_of(ci * chunk, chunk)
        y = centred(second_pad, w3_ref, r0)
        third_pad[pl.ds(bins + r0, chunk), :] = gelu(y).astype(jnp.bfloat16)
        return carry

    lax.fori_loop(0, n_chunks, layer3, 0)

    def layer4(ci, carry):
        r0 = pl.multiple_of(ci * chunk, chunk)
        y = centred(third_pad, w4_ref, r0)
        y = y + second_pad[pl.ds(bins + r0, chunk), :].astype(f32)
        feat = y.astype(jnp.bfloat16).astype(f32)
        for p in range(chunk // pair_rows):
            pair = ci * (chunk // pair_rows) + p
            slab = pair // pairs_per_slab
            within = pair % pairs_per_slab
            block = feat[p * pair_rows:(p + 1) * pair_rows, :].T
            out_ref[slab, :, within, :, :] = block.reshape(n_xl, group, pair_rows).astype(
                jnp.bfloat16)
        return carry

    lax.fori_loop(0, n_chunks, layer4, 0)


def encode_to_send(arrived, select, counts, b1, conv2_w, conv3_w, conv4_w, n_il, n_xl):
    bins = select.shape[0]
    samples = arrived.shape[1]
    steps = samples // 16
    rows = steps * bins
    width = conv2_w.shape[1]
    out_shape = jax.ShapeDtypeStruct(
        (n_il, n_xl, steps // n_il // 2, width // n_xl, 2 * bins), jnp.bfloat16)
    return pl.pallas_call(
        functools.partial(encoder_kernel, n_il, n_xl, bins),
        out_shape=out_shape,
        in_specs=[pl.BlockSpec(memory_space=pltpu.VMEM)] * 7,
        out_specs=pl.BlockSpec(memory_space=pltpu.VMEM),
        scratch_shapes=[
            pltpu.VMEM((bins, samples + 128), jnp.bfloat16),
            pltpu.VMEM((samples // 128 * bins, 256), jnp.bfloat16),
            pltpu.VMEM((bins + rows, width), jnp.bfloat16),
            pltpu.VMEM((2 * bins + rows, width), jnp.bfloat16),
            pltpu.VMEM((2 * bins + rows, width), jnp.bfloat16),
        ],
        compiler_params=pltpu.CompilerParams(vmem_limit_bytes=48 * 1024 * 1024),
    )(arrived, select, counts, b1, conv2_w, conv3_w, conv4_w)


def merge_selectors(n_xl, lanes):
    width = lanes // n_xl
    kk = jnp.arange(2 * lanes, dtype=jnp.int32)[None, :, None]
    m = jnp.arange(n_xl * lanes, dtype=jnp.int32)[None, None, :]
    bp = jnp.arange(n_xl // 2, dtype=jnp.int32)[:, None, None]
    b = 2 * bp + kk // lanes
    lane = kk % lanes
    target = (lane // width) * lanes + width * b + lane % width
    return (m == target).astype(jnp.bfloat16)


def lane_tap_matrices(weight, lanes):
    offset = jnp.arange(lanes)[:, None] - jnp.arange(lanes)[None, :] + 1
    taps = weight.reshape(weight.shape[0], 3, 3, 1, 1)
    picked = jnp.zeros((weight.shape[0], 3, lanes, lanes), jnp.float32)
    for c in range(3):
        picked = picked + jnp.where(offset == c, taps[:, :, c], jnp.float32(0.0))
    high = lax.reduce_precision(picked, exponent_bits=8, mantissa_bits=7)
    low = (picked - high).astype(jnp.bfloat16)
    return jnp.stack([high.astype(jnp.bfloat16), low], axis=2)


def receive_kernel(recv_ref, sel_ref, taps_ref, out_ref, field):
    n_a, n_b, rows_k_o, lanes = recv_ref.shape
    n_s, n_o, n_p, n_q = out_ref.shape
    n_k = rows_k_o // n_o
    n_p4 = n_p // n_a
    per_o = n_s * n_p
    f32 = jnp.float32

    def merge(a, carry):
        y = None
        for bp in range(n_b // 2):
            x = jnp.concatenate([recv_ref[a, 2 * bp], recv_ref[a, 2 * bp + 1]], axis=1)
            d = jnp.dot(x, sel_ref[bp], preferred_element_type=f32)
            y = d if y is None else y + d
        for k in range(n_k):
            for s2 in range(2):
                for p4 in range(n_p4):
                    blk = y[k * n_o:(k + 1) * n_o, (s2 * n_p4 + p4) * lanes:(s2 * n_p4 + p4 + 1) * lanes]
                    start = (2 * k + s2) * n_p + n_p4 * a + p4
                    field[pl.ds(start, n_o, stride=per_o), :] = blk
        return carry

    lax.fori_loop(0, n_a, merge, 0)

    row = lax.broadcasted_iota(jnp.int32, (per_o, n_q), 0) % n_p
    zero = jnp.zeros((per_o, n_q), f32)

    def mix(o, carry):
        f = field[pl.ds(pl.multiple_of(o * per_o, per_o), per_o), :]
        fb = f.astype(jnp.bfloat16)
        g = []
        for r in range(3):
            t = jnp.dot(fb, taps_ref[o, r, 0], preferred_element_type=f32)
            t = t + jnp.dot(fb, taps_ref[o, r, 1], preferred_element_type=f32)
            g.append(t)
        acc = f + g[1]
        acc = acc + jnp.where(row == 0, zero, pltpu.roll(g[0], 1, 0))
        acc = acc + jnp.where(row == n_p - 1, zero, pltpu.roll(g[2], per_o - 1, 0))
        out_ref[:, o] = acc.astype(out_ref.dtype).reshape(n_s, n_p, n_q)
        return carry

    lax.fori_loop(0, n_o, mix, 0)


def receive_mix(received, sel, lw, n_s, n_o, n_p, n_q):
    return pl.pallas_call(
        receive_kernel,
        out_shape=jax.ShapeDtypeStruct((n_s, n_o, n_p, n_q), jnp.bfloat16),
        in_specs=[pl.BlockSpec(memory_space=pltpu.VMEM)] * 3,
        out_specs=pl.BlockSpec(memory_space=pltpu.VMEM),
        scratch_shapes=[pltpu.VMEM((n_s * n_o * n_p, n_q), jnp.float32)],
        compiler_params=pltpu.CompilerParams(vmem_limit_bytes=48 * 1024 * 1024),
    )(received, sel, lw)


def per_device(traces, fold_ids, fold_counts, conv1_w, conv2_w, conv3_w, conv4_w, lateral_w):
    il_count = lax.axis_size("il")
    xl_count = lax.axis_size("xl")
    devices = il_count * xl_count
    rows_here = traces.shape[0]
    samples = traces.shape[1]
    bins_il, bins_xl, fold_depth = fold_ids.shape
    bin_total = bins_il * bins_xl
    slot_total = bin_total * fold_depth
    capacity = 2 * slot_total // devices
    flat_ids = fold_ids.reshape(slot_total)
    source = flat_ids // rows_here
    local_row = flat_ids % rows_here
    onehot = (source[:, None] == jnp.arange(devices, dtype=jnp.int32)[None, :]).astype(jnp.int32)
    slot_rank = jnp.sum(onehot * jnp.cumsum(onehot, axis=0), axis=1) - 1
    position = source * capacity + slot_rank
    requests = (
        jnp.zeros((devices * capacity,), jnp.int32)
        .at[position]
        .set(local_row)
        .reshape(devices, capacity)
    )
    wanted = exchange(requests, il_count, xl_count, 1)
    picked = jnp.take(traces, wanted.reshape(-1), axis=0)
    arrived = lax.all_to_all(picked, ("il", "xl"), split_axis=0, concat_axis=0, tiled=True)
    live = jnp.arange(fold_depth, dtype=jnp.int32)[None, :] < fold_counts.reshape(bin_total, 1)
    rows_in = jnp.arange(devices * capacity, dtype=jnp.int32)[None, None, :]
    select = jnp.any(
        (position.reshape(bin_total, fold_depth)[:, :, None] == rows_in) & live[:, :, None], axis=1
    ).astype(jnp.bfloat16)
    outgoing = encode_to_send(
        arrived, select, fold_counts.reshape(bin_total, 1), window_first_weights(conv1_w, 256),
        conv2_w, conv3_w, conv4_w, il_count, xl_count,
    )
    pairs = outgoing.shape[2]
    group_width = outgoing.shape[3]
    outgoing = outgoing.reshape(devices, pairs, group_width, 2 * bin_total)
    received = lax.all_to_all(outgoing, ("il", "xl"), split_axis=0, concat_axis=0, tiled=True)
    received = received.reshape(il_count, xl_count, pairs * group_width, 2 * bin_total)
    return receive_mix(
        received, merge_selectors(xl_count, 2 * bin_total),
        lane_tap_matrices(lateral_w, xl_count * bins_xl),
        2 * pairs, group_width, il_count * bins_il, xl_count * bins_xl,
    )


def solution(mesh):
    return jax.shard_map(
        per_device,
        mesh=mesh,
        in_specs=(
            P(("il", "xl"), None),
            P("il", "xl", None),
            P("il", "xl"),
            P(),
            P(),
            P(),
            P(),
            P("xl", None),
        ),
        out_specs=P("il", "xl", None, None),
        check_vma=False,
    )
```

```python
import functools

import jax
import jax.numpy as jnp
import numpy as np
from jax import lax
from jax.experimental import pallas as pl
from jax.experimental.pallas import tpu as pltpu
from jax.sharding import PartitionSpec as P


def window_first_weights(conv1_w, window):
    l_index = jnp.arange(window, dtype=jnp.int32)[None, :, None, None]
    c_index = jnp.arange(9, dtype=jnp.int32)[:, None, None, None]
    u_index = jnp.arange(4, dtype=jnp.int32)[None, None, :, None]
    tap_index = jnp.arange(8, dtype=jnp.int32)[None, None, None, :]
    start = jnp.where(c_index < 8, 16 * c_index + 12, -4)
    selector = (l_index - start - 4 * u_index == tap_index).astype(jnp.float32)
    return (
        jnp.einsum("clut,to->cluo", selector, conv1_w.astype(jnp.float32))
        .astype(jnp.bfloat16)
        .reshape(9, window, 4 * conv1_w.shape[1])
    )


MESH = pl.DeviceIdType.MESH


def exchange_kernel(n_il, n_xl, x_ref, y_ref, send_sem, recv_sem):
    n = n_il * n_xl
    me = lax.axis_index("il") * n_xl + lax.axis_index("xl")
    pltpu.make_async_copy(x_ref.at[me], y_ref.at[me], recv_sem).start()

    def send(k, carry):
        d = lax.rem(me + 1 + k, n)
        pltpu.make_async_remote_copy(
            src_ref=x_ref.at[d], dst_ref=y_ref.at[me], send_sem=send_sem, recv_sem=recv_sem,
            device_id=(d // n_xl, d % n_xl), device_id_type=MESH,
        ).start()
        return carry

    lax.fori_loop(0, n - 1, send, 0)
    pltpu.make_async_copy(y_ref, y_ref, recv_sem).wait()
    pltpu.make_async_copy(x_ref.at[pl.ds(0, n - 1)], y_ref.at[pl.ds(0, n - 1)], send_sem).wait()


def exchange(x, n_il, n_xl):
    return pl.pallas_call(
        functools.partial(exchange_kernel, n_il, n_xl),
        out_shape=jax.ShapeDtypeStruct(x.shape, x.dtype),
        in_specs=[pl.BlockSpec(memory_space=pl.ANY)],
        out_specs=pl.BlockSpec(memory_space=pl.ANY),
        scratch_shapes=[pltpu.SemaphoreType.DMA(()), pltpu.SemaphoreType.DMA(())],
        compiler_params=pltpu.CompilerParams(has_side_effects=True),
    )(x)

def encoder_kernel(n_il, n_xl, bins, arrived_ref, select_ref, counts_ref, b1_ref, w2_ref, w3_ref,
                   w4_ref, out_ref, stacked, paired, first_pad, second_pad, third_pad):
    samples = arrived_ref.shape[1]
    width = w2_ref.shape[1]
    rows = first_pad.shape[0] - bins
    chunk = 8 * bins
    n_chunks = rows // chunk
    pair_rows = 2 * bins
    group = width // n_xl
    pairs_per_slab = out_ref.shape[2]
    blocks = samples // 128
    f32 = jnp.float32

    zeros_pad = jnp.zeros((bins, width), jnp.bfloat16)
    first_pad[pl.ds(0, bins), :] = zeros_pad
    second_pad[pl.ds(0, bins), :] = zeros_pad
    second_pad[pl.ds(bins + rows, bins), :] = zeros_pad
    third_pad[pl.ds(0, bins), :] = zeros_pad
    third_pad[pl.ds(bins + rows, bins), :] = zeros_pad

    counts = counts_ref[...]
    running = jnp.dot(select_ref[...], arrived_ref[...], preferred_element_type=f32)
    stacked[:, pl.ds(0, samples)] = (running / counts.astype(f32)).astype(jnp.bfloat16)
    stacked[:, pl.ds(samples, 128)] = jnp.zeros((bins, 128), jnp.bfloat16)
    for m in range(blocks):
        paired[pl.ds(m * bins, bins), :] = stacked[:, pl.ds(m * 128, 256)]

    def gelu(x):
        return jax.nn.gelu(x)

    def layer1(c, carry):
        y = jnp.dot(paired[...], b1_ref[c], preferred_element_type=f32)
        y = gelu(y).astype(jnp.bfloat16)
        for m in range(blocks):
            step = 1 + c + 8 * m
            if m == blocks - 1:
                @pl.when(c < 7)
                def _():
                    first_pad[pl.ds(pl.multiple_of(bins + bins * step, bins), bins), :] = (
                        y[m * bins:(m + 1) * bins])
            else:
                first_pad[pl.ds(pl.multiple_of(bins + bins * step, bins), bins), :] = (
                    y[m * bins:(m + 1) * bins])
        return carry

    lax.fori_loop(0, 8, layer1, 0)
    y0 = jnp.dot(paired[pl.ds(0, bins), :], b1_ref[8], preferred_element_type=f32)
    first_pad[pl.ds(bins, bins), :] = gelu(y0).astype(jnp.bfloat16)

    def layer2(ci, carry):
        r0 = pl.multiple_of(ci * chunk, chunk)
        earlier = first_pad[pl.ds(r0, chunk), :]
        current = first_pad[pl.ds(r0 + bins, chunk), :]
        y = jnp.dot(earlier, w2_ref[pl.ds(0, width), :], preferred_element_type=f32)
        y = y + jnp.dot(current, w2_ref[pl.ds(width, width), :], preferred_element_type=f32)
        second_pad[pl.ds(bins + r0, chunk), :] = gelu(y).astype(jnp.bfloat16)
        return carry

    lax.fori_loop(0, n_chunks, layer2, 0)

    def centred(src, w_ref, r0):
        y = jnp.dot(src[pl.ds(r0, chunk), :], w_ref[pl.ds(0, width), :], preferred_element_type=f32)
        y = y + jnp.dot(src[pl.ds(r0 + bins, chunk), :], w_ref[pl.ds(width, width), :],
                        preferred_element_type=f32)
        y = y + jnp.dot(src[pl.ds(r0 + 2 * bins, chunk), :], w_ref[pl.ds(2 * width, width), :],
                        preferred_element_type=f32)
        return y

    def layer3(ci, carry):
        r0 = pl.multiple_of(ci * chunk, chunk)
        y = centred(second_pad, w3_ref, r0)
        third_pad[pl.ds(bins + r0, chunk), :] = gelu(y).astype(jnp.bfloat16)
        return carry

    lax.fori_loop(0, n_chunks, layer3, 0)

    def layer4(ci, carry):
        r0 = pl.multiple_of(ci * chunk, chunk)
        y = centred(third_pad, w4_ref, r0)
        y = y + second_pad[pl.ds(bins + r0, chunk), :].astype(f32)
        feat = y.astype(jnp.bfloat16).astype(f32)
        for p in range(chunk // pair_rows):
            pair = ci * (chunk // pair_rows) + p
            slab = pair // pairs_per_slab
            within = pair % pairs_per_slab
            block = feat[p * pair_rows:(p + 1) * pair_rows, :].T
            out_ref[slab, :, within, :, :] = block.reshape(n_xl, group, pair_rows).astype(
                jnp.bfloat16)
        return carry

    lax.fori_loop(0, n_chunks, layer4, 0)


def encode_to_send(arrived, select, counts, b1, conv2_w, conv3_w, conv4_w, n_il, n_xl):
    bins = select.shape[0]
    samples = arrived.shape[1]
    steps = samples // 16
    rows = steps * bins
    width = conv2_w.shape[1]
    out_shape = jax.ShapeDtypeStruct(
        (n_il, n_xl, steps // n_il // 2, width // n_xl, 2 * bins), jnp.bfloat16)
    return pl.pallas_call(
        functools.partial(encoder_kernel, n_il, n_xl, bins),
        out_shape=out_shape,
        in_specs=[pl.BlockSpec(memory_space=pltpu.VMEM)] * 7,
        out_specs=pl.BlockSpec(memory_space=pltpu.VMEM),
        scratch_shapes=[
            pltpu.VMEM((bins, samples + 128), jnp.bfloat16),
            pltpu.VMEM((samples // 128 * bins, 256), jnp.bfloat16),
            pltpu.VMEM((bins + rows, width), jnp.bfloat16),
            pltpu.VMEM((2 * bins + rows, width), jnp.bfloat16),
            pltpu.VMEM((2 * bins + rows, width), jnp.bfloat16),
        ],
        compiler_params=pltpu.CompilerParams(vmem_limit_bytes=48 * 1024 * 1024),
    )(arrived, select, counts, b1, conv2_w, conv3_w, conv4_w)


def merge_selectors(n_xl, lanes):
    width = lanes // n_xl
    kk = jnp.arange(2 * lanes, dtype=jnp.int32)[None, :, None]
    m = jnp.arange(n_xl * lanes, dtype=jnp.int32)[None, None, :]
    bp = jnp.arange(n_xl // 2, dtype=jnp.int32)[:, None, None]
    b = 2 * bp + kk // lanes
    lane = kk % lanes
    target = (lane // width) * lanes + width * b + lane % width
    return (m == target).astype(jnp.bfloat16)


def lane_tap_matrices(weight, lanes):
    offset = jnp.arange(lanes)[:, None] - jnp.arange(lanes)[None, :] + 1
    taps = weight.reshape(weight.shape[0], 3, 3, 1, 1)
    picked = jnp.zeros((weight.shape[0], 3, lanes, lanes), jnp.float32)
    for c in range(3):
        picked = picked + jnp.where(offset == c, taps[:, :, c], jnp.float32(0.0))
    high = lax.reduce_precision(picked, exponent_bits=8, mantissa_bits=7)
    low = (picked - high).astype(jnp.bfloat16)
    return jnp.stack([high.astype(jnp.bfloat16), low], axis=2)


def receive_kernel(recv_ref, sel_ref, taps_ref, out_ref, field):
    n_a, n_b, rows_k_o, lanes = recv_ref.shape
    n_s, n_o, n_p, n_q = out_ref.shape
    n_k = rows_k_o // n_o
    n_p4 = n_p // n_a
    per_o = n_s * n_p
    f32 = jnp.float32

    def merge(a, carry):
        y = None
        for bp in range(n_b // 2):
            x = jnp.concatenate([recv_ref[a, 2 * bp], recv_ref[a, 2 * bp + 1]], axis=1)
            d = jnp.dot(x, sel_ref[bp], preferred_element_type=f32)
            y = d if y is None else y + d
        for k in range(n_k):
            for s2 in range(2):
                for p4 in range(n_p4):
                    blk = y[k * n_o:(k + 1) * n_o, (s2 * n_p4 + p4) * lanes:(s2 * n_p4 + p4 + 1) * lanes]
                    start = (2 * k + s2) * n_p + n_p4 * a + p4
                    field[pl.ds(start, n_o, stride=per_o), :] = blk
        return carry

    lax.fori_loop(0, n_a, merge, 0)

    row = lax.broadcasted_iota(jnp.int32, (per_o, n_q), 0) % n_p
    zero = jnp.zeros((per_o, n_q), f32)

    def mix(o, carry):
        f = field[pl.ds(pl.multiple_of(o * per_o, per_o), per_o), :]
        fb = f.astype(jnp.bfloat16)
        g = []
        for r in range(3):
            t = jnp.dot(fb, taps_ref[o, r, 0], preferred_element_type=f32)
            t = t + jnp.dot(fb, taps_ref[o, r, 1], preferred_element_type=f32)
            g.append(t)
        acc = f + g[1]
        acc = acc + jnp.where(row == 0, zero, pltpu.roll(g[0], 1, 0))
        acc = acc + jnp.where(row == n_p - 1, zero, pltpu.roll(g[2], per_o - 1, 0))
        out_ref[:, o] = acc.astype(out_ref.dtype).reshape(n_s, n_p, n_q)
        return carry

    lax.fori_loop(0, n_o, mix, 0)


def receive_mix(received, sel, lw, n_s, n_o, n_p, n_q):
    return pl.pallas_call(
        receive_kernel,
        out_shape=jax.ShapeDtypeStruct((n_s, n_o, n_p, n_q), jnp.bfloat16),
        in_specs=[pl.BlockSpec(memory_space=pltpu.VMEM)] * 3,
        out_specs=pl.BlockSpec(memory_space=pltpu.VMEM),
        scratch_shapes=[pltpu.VMEM((n_s * n_o * n_p, n_q), jnp.float32)],
        compiler_params=pltpu.CompilerParams(vmem_limit_bytes=48 * 1024 * 1024),
    )(received, sel, lw)


def per_device(traces, fold_ids, fold_counts, conv1_w, conv2_w, conv3_w, conv4_w, lateral_w):
    il_count = lax.axis_size("il")
    xl_count = lax.axis_size("xl")
    devices = il_count * xl_count
    rows_here = traces.shape[0]
    samples = traces.shape[1]
    bins_il, bins_xl, fold_depth = fold_ids.shape
    bin_total = bins_il * bins_xl
    slot_total = bin_total * fold_depth
    capacity = 2 * slot_total // devices
    flat_ids = fold_ids.reshape(slot_total)
    source = flat_ids // rows_here
    local_row = flat_ids % rows_here
    onehot = (source[:, None] == jnp.arange(devices, dtype=jnp.int32)[None, :]).astype(jnp.int32)
    slot_rank = jnp.sum(onehot * jnp.cumsum(onehot, axis=0), axis=1) - 1
    position = source * capacity + slot_rank
    requests = (
        jnp.zeros((devices * capacity,), jnp.int32)
        .at[position]
        .set(local_row)
        .reshape(devices, capacity)
    )
    wanted = exchange(requests, il_count, xl_count)
    picked = jnp.take(traces, wanted.reshape(-1), axis=0)
    arrived = lax.all_to_all(picked, ("il", "xl"), split_axis=0, concat_axis=0, tiled=True)
    live = jnp.arange(fold_depth, dtype=jnp.int32)[None, :] < fold_counts.reshape(bin_total, 1)
    rows_in = jnp.arange(devices * capacity, dtype=jnp.int32)[None, None, :]
    select = jnp.any(
        (position.reshape(bin_total, fold_depth)[:, :, None] == rows_in) & live[:, :, None], axis=1
    ).astype(jnp.bfloat16)
    outgoing = encode_to_send(
        arrived, select, fold_counts.reshape(bin_total, 1), window_first_weights(conv1_w, 256),
        conv2_w, conv3_w, conv4_w, il_count, xl_count,
    )
    pairs = outgoing.shape[2]
    group_width = outgoing.shape[3]
    outgoing = outgoing.reshape(devices, pairs, group_width, 2 * bin_total)
    received = lax.all_to_all(outgoing, ("il", "xl"), split_axis=0, concat_axis=0, tiled=True)
    received = received.reshape(il_count, xl_count, pairs * group_width, 2 * bin_total)
    return receive_mix(
        received, merge_selectors(xl_count, 2 * bin_total),
        lane_tap_matrices(lateral_w, xl_count * bins_xl),
        2 * pairs, group_width, il_count * bins_il, xl_count * bins_xl,
    )


def solution(mesh):
    return jax.shard_map(
        per_device,
        mesh=mesh,
        in_specs=(
            P(("il", "xl"), None),
            P("il", "xl", None),
            P("il", "xl"),
            P(),
            P(),
            P(),
            P(),
            P("xl", None),
        ),
        out_specs=P("il", "xl", None, None),
        check_vma=False,
    )
```

```python
import functools

import jax
import jax.numpy as jnp
import numpy as np
from jax import lax
from jax.experimental import pallas as pl
from jax.experimental.pallas import tpu as pltpu
from jax.sharding import PartitionSpec as P


def window_first_weights(conv1_w, window):
    l_index = jnp.arange(window, dtype=jnp.int32)[None, :, None, None]
    c_index = jnp.arange(9, dtype=jnp.int32)[:, None, None, None]
    u_index = jnp.arange(4, dtype=jnp.int32)[None, None, :, None]
    tap_index = jnp.arange(8, dtype=jnp.int32)[None, None, None, :]
    start = jnp.where(c_index < 8, 16 * c_index + 12, -4)
    selector = (l_index - start - 4 * u_index == tap_index).astype(jnp.float32)
    return (
        jnp.einsum("clut,to->cluo", selector, conv1_w.astype(jnp.float32))
        .astype(jnp.bfloat16)
        .reshape(9, window, 4 * conv1_w.shape[1])
    )


MESH = pl.DeviceIdType.MESH


def exchange_kernel(n_il, n_xl, x_ref, y_ref, send_sem, recv_sem):
    n = n_il * n_xl
    me = lax.axis_index("il") * n_xl + lax.axis_index("xl")
    barrier = pltpu.get_barrier_semaphore()

    def greet(k, carry):
        d = lax.rem(me + 1 + k, n)
        pl.semaphore_signal(barrier, inc=1, device_id=(d // n_xl, d % n_xl), device_id_type=MESH)
        return carry

    lax.fori_loop(0, n - 1, greet, 0)
    pl.semaphore_wait(barrier, n - 1)
    pltpu.make_async_copy(x_ref.at[me], y_ref.at[me], recv_sem).start()

    def send(k, carry):
        d = lax.rem(me + 1 + k, n)
        pltpu.make_async_remote_copy(
            src_ref=x_ref.at[d], dst_ref=y_ref.at[me], send_sem=send_sem, recv_sem=recv_sem,
            device_id=(d // n_xl, d % n_xl), device_id_type=MESH,
        ).start()
        return carry

    lax.fori_loop(0, n - 1, send, 0)
    pltpu.make_async_copy(y_ref, y_ref, recv_sem).wait()
    pltpu.make_async_copy(x_ref.at[pl.ds(0, n - 1)], y_ref.at[pl.ds(0, n - 1)], send_sem).wait()


def exchange(x, n_il, n_xl, collective_id):
    return pl.pallas_call(
        functools.partial(exchange_kernel, n_il, n_xl),
        out_shape=jax.ShapeDtypeStruct(x.shape, x.dtype),
        in_specs=[pl.BlockSpec(memory_space=pl.ANY)],
        out_specs=pl.BlockSpec(memory_space=pl.ANY),
        scratch_shapes=[pltpu.SemaphoreType.DMA(()), pltpu.SemaphoreType.DMA(())],
        compiler_params=pltpu.CompilerParams(collective_id=collective_id, has_side_effects=True),
    )(x)

def encoder_kernel(n_il, n_xl, bins, arrived_ref, select_ref, counts_ref, b1_ref, w2_ref, w3_ref,
                   w4_ref, out_ref, stacked, paired, first_pad, second_pad, third_pad):
    samples = arrived_ref.shape[1]
    width = w2_ref.shape[1]
    rows = first_pad.shape[0] - bins
    chunk = 8 * bins
    n_chunks = rows // chunk
    pair_rows = 2 * bins
    group = width // n_xl
    pairs_per_slab = out_ref.shape[2]
    blocks = samples // 128
    f32 = jnp.float32

    zeros_pad = jnp.zeros((bins, width), jnp.bfloat16)
    first_pad[pl.ds(0, bins), :] = zeros_pad
    second_pad[pl.ds(0, bins), :] = zeros_pad
    second_pad[pl.ds(bins + rows, bins), :] = zeros_pad
    third_pad[pl.ds(0, bins), :] = zeros_pad
    third_pad[pl.ds(bins + rows, bins), :] = zeros_pad

    counts = counts_ref[...]
    running = jnp.dot(select_ref[...], arrived_ref[...], preferred_element_type=f32)
    stacked[:, pl.ds(0, samples)] = (running / counts.astype(f32)).astype(jnp.bfloat16)
    stacked[:, pl.ds(samples, 128)] = jnp.zeros((bins, 128), jnp.bfloat16)
    for m in range(blocks):
        paired[pl.ds(m * bins, bins), :] = stacked[:, pl.ds(m * 128, 256)]

    def gelu(x):
        return jax.nn.gelu(x)

    def layer1(c, carry):
        y = jnp.dot(paired[...], b1_ref[c], preferred_element_type=f32)
        y = gelu(y).astype(jnp.bfloat16)
        for m in range(blocks):
            step = 1 + c + 8 * m
            if m == blocks - 1:
                @pl.when(c < 7)
                def _():
                    first_pad[pl.ds(pl.multiple_of(bins + bins * step, bins), bins), :] = (
                        y[m * bins:(m + 1) * bins])
            else:
                first_pad[pl.ds(pl.multiple_of(bins + bins * step, bins), bins), :] = (
                    y[m * bins:(m + 1) * bins])
        return carry

    lax.fori_loop(0, 8, layer1, 0)
    y0 = jnp.dot(paired[pl.ds(0, bins), :], b1_ref[8], preferred_element_type=f32)
    first_pad[pl.ds(bins, bins), :] = gelu(y0).astype(jnp.bfloat16)

    def layer2(ci, carry):
        r0 = pl.multiple_of(ci * chunk, chunk)
        earlier = first_pad[pl.ds(r0, chunk), :]
        current = first_pad[pl.ds(r0 + bins, chunk), :]
        y = jnp.dot(earlier, w2_ref[pl.ds(0, width), :], preferred_element_type=f32)
        y = y + jnp.dot(current, w2_ref[pl.ds(width, width), :], preferred_element_type=f32)
        second_pad[pl.ds(bins + r0, chunk), :] = gelu(y).astype(jnp.bfloat16)
        return carry

    lax.fori_loop(0, n_chunks, layer2, 0)

    def centred(src, w_ref, r0):
        y = jnp.dot(src[pl.ds(r0, chunk), :], w_ref[pl.ds(0, width), :], preferred_element_type=f32)
        y = y + jnp.dot(src[pl.ds(r0 + bins, chunk), :], w_ref[pl.ds(width, width), :],
                        preferred_element_type=f32)
        y = y + jnp.dot(src[pl.ds(r0 + 2 * bins, chunk), :], w_ref[pl.ds(2 * width, width), :],
                        preferred_element_type=f32)
        return y

    def layer3(ci, carry):
        r0 = pl.multiple_of(ci * chunk, chunk)
        y = centred(second_pad, w3_ref, r0)
        third_pad[pl.ds(bins + r0, chunk), :] = gelu(y).astype(jnp.bfloat16)
        return carry

    lax.fori_loop(0, n_chunks, layer3, 0)

    def layer4(ci, carry):
        r0 = pl.multiple_of(ci * chunk, chunk)
        y = centred(third_pad, w4_ref, r0)
        y = y + second_pad[pl.ds(bins + r0, chunk), :].astype(f32)
        feat = y.astype(jnp.bfloat16).astype(f32)
        for p in range(chunk // pair_rows):
            pair = ci * (chunk // pair_rows) + p
            slab = pair // pairs_per_slab
            within = pair % pairs_per_slab
            block = feat[p * pair_rows:(p + 1) * pair_rows, :].T
            out_ref[slab, :, within, :, :] = block.reshape(n_xl, group, pair_rows).astype(
                jnp.bfloat16)
        return carry

    lax.fori_loop(0, n_chunks, layer4, 0)


def encode_to_send(arrived, select, counts, b1, conv2_w, conv3_w, conv4_w, n_il, n_xl):
    bins = select.shape[0]
    samples = arrived.shape[1]
    steps = samples // 16
    rows = steps * bins
    width = conv2_w.shape[1]
    out_shape = jax.ShapeDtypeStruct(
        (n_il, n_xl, steps // n_il // 2, width // n_xl, 2 * bins), jnp.bfloat16)
    return pl.pallas_call(
        functools.partial(encoder_kernel, n_il, n_xl, bins),
        out_shape=out_shape,
        in_specs=[pl.BlockSpec(memory_space=pltpu.VMEM)] * 7,
        out_specs=pl.BlockSpec(memory_space=pltpu.VMEM),
        scratch_shapes=[
            pltpu.VMEM((bins, samples + 128), jnp.bfloat16),
            pltpu.VMEM((samples // 128 * bins, 256), jnp.bfloat16),
            pltpu.VMEM((bins + rows, width), jnp.bfloat16),
            pltpu.VMEM((2 * bins + rows, width), jnp.bfloat16),
            pltpu.VMEM((2 * bins + rows, width), jnp.bfloat16),
        ],
        compiler_params=pltpu.CompilerParams(vmem_limit_bytes=48 * 1024 * 1024),
    )(arrived, select, counts, b1, conv2_w, conv3_w, conv4_w)


def merge_selectors(n_xl, lanes):
    width = lanes // n_xl
    kk = jnp.arange(2 * lanes, dtype=jnp.int32)[None, :, None]
    m = jnp.arange(n_xl * lanes, dtype=jnp.int32)[None, None, :]
    bp = jnp.arange(n_xl // 2, dtype=jnp.int32)[:, None, None]
    b = 2 * bp + kk // lanes
    lane = kk % lanes
    target = (lane // width) * lanes + width * b + lane % width
    return (m == target).astype(jnp.bfloat16)


def lane_tap_matrices(weight, lanes):
    offset = jnp.arange(lanes)[:, None] - jnp.arange(lanes)[None, :] + 1
    taps = weight.reshape(weight.shape[0], 3, 3, 1, 1)
    picked = jnp.zeros((weight.shape[0], 3, lanes, lanes), jnp.float32)
    for c in range(3):
        picked = picked + jnp.where(offset == c, taps[:, :, c], jnp.float32(0.0))
    high = lax.reduce_precision(picked, exponent_bits=8, mantissa_bits=7)
    low = (picked - high).astype(jnp.bfloat16)
    return jnp.stack([high.astype(jnp.bfloat16), low], axis=2)


def receive_kernel(recv_ref, sel_ref, taps_ref, out_ref, field):
    n_a, n_b, rows_k_o, lanes = recv_ref.shape
    n_s, n_o, n_p, n_q = out_ref.shape
    n_k = rows_k_o // n_o
    n_p4 = n_p // n_a
    per_o = n_s * n_p
    f32 = jnp.float32

    def merge(a, carry):
        y = None
        for bp in range(n_b // 2):
            x = jnp.concatenate([recv_ref[a, 2 * bp], recv_ref[a, 2 * bp + 1]], axis=1)
            d = jnp.dot(x, sel_ref[bp], preferred_element_type=f32)
            y = d if y is None else y + d
        for k in range(n_k):
            for s2 in range(2):
                for p4 in range(n_p4):
                    blk = y[k * n_o:(k + 1) * n_o, (s2 * n_p4 + p4) * lanes:(s2 * n_p4 + p4 + 1) * lanes]
                    start = (2 * k + s2) * n_p + n_p4 * a + p4
                    field[pl.ds(start, n_o, stride=per_o), :] = blk
        return carry

    lax.fori_loop(0, n_a, merge, 0)

    row = lax.broadcasted_iota(jnp.int32, (per_o, n_q), 0) % n_p
    zero = jnp.zeros((per_o, n_q), f32)

    def mix(o, carry):
        f = field[pl.ds(pl.multiple_of(o * per_o, per_o), per_o), :]
        fb = f.astype(jnp.bfloat16)
        g = []
        for r in range(3):
            t = jnp.dot(fb, taps_ref[o, r, 0], preferred_element_type=f32)
            t = t + jnp.dot(fb, taps_ref[o, r, 1], preferred_element_type=f32)
            g.append(t)
        acc = f + g[1]
        acc = acc + jnp.where(row == 0, zero, pltpu.roll(g[0], 1, 0))
        acc = acc + jnp.where(row == n_p - 1, zero, pltpu.roll(g[2], per_o - 1, 0))
        out_ref[:, o] = acc.astype(out_ref.dtype).reshape(n_s, n_p, n_q)
        return carry

    lax.fori_loop(0, n_o, mix, 0)


def receive_mix(received, sel, lw, n_s, n_o, n_p, n_q):
    return pl.pallas_call(
        receive_kernel,
        out_shape=jax.ShapeDtypeStruct((n_s, n_o, n_p, n_q), jnp.bfloat16),
        in_specs=[pl.BlockSpec(memory_space=pltpu.VMEM)] * 3,
        out_specs=pl.BlockSpec(memory_space=pltpu.VMEM),
        scratch_shapes=[pltpu.VMEM((n_s * n_o * n_p, n_q), jnp.float32)],
        compiler_params=pltpu.CompilerParams(vmem_limit_bytes=48 * 1024 * 1024),
    )(received, sel, lw)


def per_device(traces, fold_ids, fold_counts, conv1_w, conv2_w, conv3_w, conv4_w, lateral_w):
    il_count = lax.axis_size("il")
    xl_count = lax.axis_size("xl")
    devices = il_count * xl_count
    rows_here = traces.shape[0]
    samples = traces.shape[1]
    bins_il, bins_xl, fold_depth = fold_ids.shape
    bin_total = bins_il * bins_xl
    slot_total = bin_total * fold_depth
    capacity = 2 * slot_total // devices
    flat_ids = fold_ids.reshape(slot_total)
    source = flat_ids // rows_here
    local_row = flat_ids % rows_here
    onehot = (source[:, None] == jnp.arange(devices, dtype=jnp.int32)[None, :]).astype(jnp.int32)
    slot_rank = jnp.sum(onehot * jnp.cumsum(onehot, axis=0), axis=1) - 1
    position = source * capacity + slot_rank
    requests = (
        jnp.zeros((devices * capacity,), jnp.int32)
        .at[position]
        .set(local_row, mode="promise_in_bounds", unique_indices=True)
        .reshape(devices, capacity)
    )
    wanted = exchange(requests, il_count, xl_count, 1)
    picked = jnp.take(traces, wanted, axis=0, mode="clip")
    arrived = lax.all_to_all(picked, ("il", "xl"), split_axis=0, concat_axis=0, tiled=True)
    arrived = arrived.reshape(devices * capacity, samples)
    live = jnp.arange(fold_depth, dtype=jnp.int32)[None, :] < fold_counts.reshape(bin_total, 1)
    rows_in = jnp.arange(devices * capacity, dtype=jnp.int32)[None, None, :]
    select = jnp.any(
        (position.reshape(bin_total, fold_depth)[:, :, None] == rows_in) & live[:, :, None], axis=1
    ).astype(jnp.bfloat16)
    outgoing = encode_to_send(
        arrived, select, fold_counts.reshape(bin_total, 1), window_first_weights(conv1_w, 256),
        conv2_w, conv3_w, conv4_w, il_count, xl_count,
    )
    pairs = outgoing.shape[2]
    group_width = outgoing.shape[3]
    outgoing = outgoing.reshape(devices, pairs, group_width, 2 * bin_total)
    received = lax.all_to_all(outgoing, ("il", "xl"), split_axis=0, concat_axis=0, tiled=True)
    received = received.reshape(il_count, xl_count, pairs * group_width, 2 * bin_total)
    return receive_mix(
        received, merge_selectors(xl_count, 2 * bin_total),
        lane_tap_matrices(lateral_w, xl_count * bins_xl),
        2 * pairs, group_width, il_count * bins_il, xl_count * bins_xl,
    )


def solution(mesh):
    return jax.shard_map(
        per_device,
        mesh=mesh,
        in_specs=(
            P(("il", "xl"), None),
            P("il", "xl", None),
            P("il", "xl"),
            P(),
            P(),
            P(),
            P(),
            P("xl", None),
        ),
        out_specs=P("il", "xl", None, None),
        check_vma=False,
    )
```

```python
import functools

import jax
import jax.numpy as jnp
import numpy as np
from jax import lax
from jax.experimental import pallas as pl
from jax.experimental.pallas import tpu as pltpu
from jax.sharding import PartitionSpec as P


def window_first_weights(conv1_w, window):
    l_index = jnp.arange(window, dtype=jnp.int32)[None, :, None, None]
    c_index = jnp.arange(9, dtype=jnp.int32)[:, None, None, None]
    u_index = jnp.arange(4, dtype=jnp.int32)[None, None, :, None]
    tap_index = jnp.arange(8, dtype=jnp.int32)[None, None, None, :]
    start = jnp.where(c_index < 8, 16 * c_index + 12, -4)
    selector = (l_index - start - 4 * u_index == tap_index).astype(jnp.float32)
    return (
        jnp.einsum("clut,to->cluo", selector, conv1_w.astype(jnp.float32))
        .astype(jnp.bfloat16)
        .reshape(9, window, 4 * conv1_w.shape[1])
    )


MESH = pl.DeviceIdType.MESH


def exchange_kernel(n_il, n_xl, x_ref, y_ref, send_sem, recv_sem):
    n = n_il * n_xl
    me = lax.axis_index("il") * n_xl + lax.axis_index("xl")
    barrier = pltpu.get_barrier_semaphore()

    def greet(k, carry):
        d = lax.rem(me + 1 + k, n)
        pl.semaphore_signal(barrier, inc=1, device_id=(d // n_xl, d % n_xl), device_id_type=MESH)
        return carry

    lax.fori_loop(0, n - 1, greet, 0)
    pl.semaphore_wait(barrier, n - 1)
    pltpu.make_async_copy(x_ref.at[me], y_ref.at[me], recv_sem).start()

    def send(k, carry):
        d = lax.rem(me + 1 + k, n)
        pltpu.make_async_remote_copy(
            src_ref=x_ref.at[d], dst_ref=y_ref.at[me], send_sem=send_sem, recv_sem=recv_sem,
            device_id=(d // n_xl, d % n_xl), device_id_type=MESH,
        ).start()
        return carry

    lax.fori_loop(0, n - 1, send, 0)
    pltpu.make_async_copy(y_ref, y_ref, recv_sem).wait()
    pltpu.make_async_copy(x_ref.at[pl.ds(0, n - 1)], y_ref.at[pl.ds(0, n - 1)], send_sem).wait()


def exchange(x, n_il, n_xl, collective_id):
    return pl.pallas_call(
        functools.partial(exchange_kernel, n_il, n_xl),
        out_shape=jax.ShapeDtypeStruct(x.shape, x.dtype),
        in_specs=[pl.BlockSpec(memory_space=pl.ANY)],
        out_specs=pl.BlockSpec(memory_space=pl.ANY),
        scratch_shapes=[pltpu.SemaphoreType.DMA(()), pltpu.SemaphoreType.DMA(())],
        compiler_params=pltpu.CompilerParams(collective_id=collective_id, has_side_effects=True),
    )(x)

def encoder_kernel(n_il, n_xl, bins, arrived_ref, select_ref, counts_ref, b1_hbm, w2_hbm, w3_hbm,
                   w4_hbm, out_ref, stacked, paired, first_pad, second_pad, third_pad,
                   b1_ref, w2_ref, w3_ref, w4_ref, weight_sems):
    loads = [
        pltpu.make_async_copy(src, dst, weight_sems.at[i])
        for i, (src, dst) in enumerate(
            ((b1_hbm, b1_ref), (w2_hbm, w2_ref), (w3_hbm, w3_ref), (w4_hbm, w4_ref)))
    ]
    for load in loads:
        load.start()
    samples = arrived_ref.shape[1]
    width = w2_ref.shape[1]
    rows = first_pad.shape[0] - bins
    chunk = 8 * bins
    n_chunks = rows // chunk
    pair_rows = 2 * bins
    group = width // n_xl
    pairs_per_slab = out_ref.shape[2]
    blocks = samples // 128
    f32 = jnp.float32

    zeros_pad = jnp.zeros((bins, width), jnp.bfloat16)
    first_pad[pl.ds(0, bins), :] = zeros_pad
    second_pad[pl.ds(0, bins), :] = zeros_pad
    second_pad[pl.ds(bins + rows, bins), :] = zeros_pad
    third_pad[pl.ds(0, bins), :] = zeros_pad
    third_pad[pl.ds(bins + rows, bins), :] = zeros_pad

    counts = counts_ref[...]
    running = jnp.dot(select_ref[...], arrived_ref[...], preferred_element_type=f32)
    stacked[:, pl.ds(0, samples)] = (running / counts.astype(f32)).astype(jnp.bfloat16)
    stacked[:, pl.ds(samples, 128)] = jnp.zeros((bins, 128), jnp.bfloat16)
    for m in range(blocks):
        paired[pl.ds(m * bins, bins), :] = stacked[:, pl.ds(m * 128, 256)]

    def gelu(x):
        return jax.nn.gelu(x)

    def layer1(c, carry):
        y = jnp.dot(paired[...], b1_ref[c], preferred_element_type=f32)
        y = gelu(y).astype(jnp.bfloat16)
        for m in range(blocks):
            step = 1 + c + 8 * m
            if m == blocks - 1:
                @pl.when(c < 7)
                def _():
                    first_pad[pl.ds(pl.multiple_of(bins + bins * step, bins), bins), :] = (
                        y[m * bins:(m + 1) * bins])
            else:
                first_pad[pl.ds(pl.multiple_of(bins + bins * step, bins), bins), :] = (
                    y[m * bins:(m + 1) * bins])
        return carry

    loads[0].wait()
    lax.fori_loop(0, 8, layer1, 0)
    y0 = jnp.dot(paired[pl.ds(0, bins), :], b1_ref[8], preferred_element_type=f32)
    first_pad[pl.ds(bins, bins), :] = gelu(y0).astype(jnp.bfloat16)

    def layer2(ci, carry):
        r0 = pl.multiple_of(ci * chunk, chunk)
        earlier = first_pad[pl.ds(r0, chunk), :]
        current = first_pad[pl.ds(r0 + bins, chunk), :]
        y = jnp.dot(earlier, w2_ref[pl.ds(0, width), :], preferred_element_type=f32)
        y = y + jnp.dot(current, w2_ref[pl.ds(width, width), :], preferred_element_type=f32)
        second_pad[pl.ds(bins + r0, chunk), :] = gelu(y).astype(jnp.bfloat16)
        return carry

    loads[1].wait()
    lax.fori_loop(0, n_chunks, layer2, 0)

    def centred(src, w_ref, r0):
        y = jnp.dot(src[pl.ds(r0, chunk), :], w_ref[pl.ds(0, width), :], preferred_element_type=f32)
        y = y + jnp.dot(src[pl.ds(r0 + bins, chunk), :], w_ref[pl.ds(width, width), :],
                        preferred_element_type=f32)
        y = y + jnp.dot(src[pl.ds(r0 + 2 * bins, chunk), :], w_ref[pl.ds(2 * width, width), :],
                        preferred_element_type=f32)
        return y

    def layer3(ci, carry):
        r0 = pl.multiple_of(ci * chunk, chunk)
        y = centred(second_pad, w3_ref, r0)
        third_pad[pl.ds(bins + r0, chunk), :] = gelu(y).astype(jnp.bfloat16)
        return carry

    loads[2].wait()
    lax.fori_loop(0, n_chunks, layer3, 0)

    def layer4(ci, carry):
        r0 = pl.multiple_of(ci * chunk, chunk)
        y = centred(third_pad, w4_ref, r0)
        y = y + second_pad[pl.ds(bins + r0, chunk), :].astype(f32)
        feat = y.astype(jnp.bfloat16).astype(f32)
        for p in range(chunk // pair_rows):
            pair = ci * (chunk // pair_rows) + p
            slab = pair // pairs_per_slab
            within = pair % pairs_per_slab
            block = feat[p * pair_rows:(p + 1) * pair_rows, :].T
            out_ref[slab, :, within, :, :] = block.reshape(n_xl, group, pair_rows).astype(
                jnp.bfloat16)
        return carry

    loads[3].wait()
    lax.fori_loop(0, n_chunks, layer4, 0)


def encode_to_send(arrived, select, counts, b1, conv2_w, conv3_w, conv4_w, n_il, n_xl):
    bins = select.shape[0]
    samples = arrived.shape[1]
    steps = samples // 16
    rows = steps * bins
    width = conv2_w.shape[1]
    out_shape = jax.ShapeDtypeStruct(
        (n_il, n_xl, steps // n_il // 2, width // n_xl, 2 * bins), jnp.bfloat16)
    return pl.pallas_call(
        functools.partial(encoder_kernel, n_il, n_xl, bins),
        out_shape=out_shape,
        in_specs=[pl.BlockSpec(memory_space=pltpu.VMEM)] * 3 + [pl.BlockSpec(memory_space=pl.ANY)] * 4,
        out_specs=pl.BlockSpec(memory_space=pltpu.VMEM),
        scratch_shapes=[
            pltpu.VMEM((bins, samples + 128), jnp.bfloat16),
            pltpu.VMEM((samples // 128 * bins, 256), jnp.bfloat16),
            pltpu.VMEM((bins + rows, width), jnp.bfloat16),
            pltpu.VMEM((2 * bins + rows, width), jnp.bfloat16),
            pltpu.VMEM((2 * bins + rows, width), jnp.bfloat16),
            pltpu.VMEM(b1.shape, b1.dtype),
            pltpu.VMEM(conv2_w.shape, conv2_w.dtype),
            pltpu.VMEM(conv3_w.shape, conv3_w.dtype),
            pltpu.VMEM(conv4_w.shape, conv4_w.dtype),
            pltpu.SemaphoreType.DMA((4,)),
        ],
        compiler_params=pltpu.CompilerParams(vmem_limit_bytes=48 * 1024 * 1024),
    )(arrived, select, counts, b1, conv2_w, conv3_w, conv4_w)


def merge_selectors(n_xl, lanes):
    width = lanes // n_xl
    kk = jnp.arange(2 * lanes, dtype=jnp.int32)[None, :, None]
    m = jnp.arange(n_xl * lanes, dtype=jnp.int32)[None, None, :]
    bp = jnp.arange(n_xl // 2, dtype=jnp.int32)[:, None, None]
    b = 2 * bp + kk // lanes
    lane = kk % lanes
    target = (lane // width) * lanes + width * b + lane % width
    return (m == target).astype(jnp.bfloat16)


def lane_tap_matrices(weight, lanes):
    offset = jnp.arange(lanes)[:, None] - jnp.arange(lanes)[None, :] + 1
    taps = weight.reshape(weight.shape[0], 3, 3, 1, 1)
    picked = jnp.zeros((weight.shape[0], 3, lanes, lanes), jnp.float32)
    for c in range(3):
        picked = picked + jnp.where(offset == c, taps[:, :, c], jnp.float32(0.0))
    high = lax.reduce_precision(picked, exponent_bits=8, mantissa_bits=7)
    low = (picked - high).astype(jnp.bfloat16)
    return jnp.stack([high.astype(jnp.bfloat16), low], axis=2)


def receive_kernel(recv_ref, sel_ref, taps_hbm, out_ref, field, taps_ref, taps_sem):
    taps_load = pltpu.make_async_copy(taps_hbm, taps_ref, taps_sem)
    taps_load.start()
    n_a, n_b, rows_k_o, lanes = recv_ref.shape
    n_s, n_o, n_p, n_q = out_ref.shape
    n_k = rows_k_o // n_o
    n_p4 = n_p // n_a
    per_o = n_s * n_p
    f32 = jnp.float32

    def merge(a, carry):
        y = None
        for bp in range(n_b // 2):
            x = jnp.concatenate([recv_ref[a, 2 * bp], recv_ref[a, 2 * bp + 1]], axis=1)
            d = jnp.dot(x, sel_ref[bp], preferred_element_type=f32)
            y = d if y is None else y + d
        for k in range(n_k):
            for s2 in range(2):
                for p4 in range(n_p4):
                    blk = y[k * n_o:(k + 1) * n_o, (s2 * n_p4 + p4) * lanes:(s2 * n_p4 + p4 + 1) * lanes]
                    start = (2 * k + s2) * n_p + n_p4 * a + p4
                    field[pl.ds(start, n_o, stride=per_o), :] = blk
        return carry

    lax.fori_loop(0, n_a, merge, 0)

    row = lax.broadcasted_iota(jnp.int32, (per_o, n_q), 0) % n_p
    zero = jnp.zeros((per_o, n_q), f32)

    def mix(o, carry):
        f = field[pl.ds(pl.multiple_of(o * per_o, per_o), per_o), :]
        fb = f.astype(jnp.bfloat16)
        g = []
        for r in range(3):
            t = jnp.dot(fb, taps_ref[o, r, 0], preferred_element_type=f32)
            t = t + jnp.dot(fb, taps_ref[o, r, 1], preferred_element_type=f32)
            g.append(t)
        acc = f + g[1]
        acc = acc + jnp.where(row == 0, zero, pltpu.roll(g[0], 1, 0))
        acc = acc + jnp.where(row == n_p - 1, zero, pltpu.roll(g[2], per_o - 1, 0))
        out_ref[:, o] = acc.astype(out_ref.dtype).reshape(n_s, n_p, n_q)
        return carry

    taps_load.wait()
    lax.fori_loop(0, n_o, mix, 0)


def receive_mix(received, sel, lw, n_s, n_o, n_p, n_q):
    return pl.pallas_call(
        receive_kernel,
        out_shape=jax.ShapeDtypeStruct((n_s, n_o, n_p, n_q), jnp.bfloat16),
        in_specs=[pl.BlockSpec(memory_space=pltpu.VMEM)] * 2 + [pl.BlockSpec(memory_space=pl.ANY)],
        out_specs=pl.BlockSpec(memory_space=pltpu.VMEM),
        scratch_shapes=[
            pltpu.VMEM((n_s * n_o * n_p, n_q), jnp.float32),
            pltpu.VMEM(lw.shape, lw.dtype),
            pltpu.SemaphoreType.DMA(()),
        ],
        compiler_params=pltpu.CompilerParams(vmem_limit_bytes=48 * 1024 * 1024),
    )(received, sel, lw)


def per_device(traces, fold_ids, fold_counts, conv1_w, conv2_w, conv3_w, conv4_w, lateral_w):
    il_count = lax.axis_size("il")
    xl_count = lax.axis_size("xl")
    devices = il_count * xl_count
    rows_here = traces.shape[0]
    samples = traces.shape[1]
    bins_il, bins_xl, fold_depth = fold_ids.shape
    bin_total = bins_il * bins_xl
    slot_total = bin_total * fold_depth
    capacity = 2 * slot_total // devices
    flat_ids = fold_ids.reshape(slot_total)
    source = flat_ids // rows_here
    local_row = flat_ids % rows_here
    onehot = (source[:, None] == jnp.arange(devices, dtype=jnp.int32)[None, :]).astype(jnp.int32)
    slot_rank = jnp.sum(onehot * jnp.cumsum(onehot, axis=0), axis=1) - 1
    position = source * capacity + slot_rank
    requests = (
        jnp.zeros((devices * capacity,), jnp.int32)
        .at[position]
        .set(local_row, mode="promise_in_bounds", unique_indices=True)
        .reshape(devices, capacity)
    )
    wanted = exchange(requests, il_count, xl_count, 1)
    picked = jnp.take(traces, wanted, axis=0, mode="clip")
    arrived = lax.all_to_all(picked, ("il", "xl"), split_axis=0, concat_axis=0, tiled=True)
    arrived = arrived.reshape(devices * capacity, samples)
    live = jnp.arange(fold_depth, dtype=jnp.int32)[None, :] < fold_counts.reshape(bin_total, 1)
    rows_in = jnp.arange(devices * capacity, dtype=jnp.int32)[None, None, :]
    select = jnp.any(
        (position.reshape(bin_total, fold_depth)[:, :, None] == rows_in) & live[:, :, None], axis=1
    ).astype(jnp.bfloat16)
    outgoing = encode_to_send(
        arrived, select, fold_counts.reshape(bin_total, 1), window_first_weights(conv1_w, 256),
        conv2_w, conv3_w, conv4_w, il_count, xl_count,
    )
    pairs = outgoing.shape[2]
    group_width = outgoing.shape[3]
    outgoing = outgoing.reshape(devices, pairs, group_width, 2 * bin_total)
    received = lax.all_to_all(outgoing, ("il", "xl"), split_axis=0, concat_axis=0, tiled=True)
    received = received.reshape(il_count, xl_count, pairs * group_width, 2 * bin_total)
    return receive_mix(
        received, merge_selectors(xl_count, 2 * bin_total),
        lane_tap_matrices(lateral_w, xl_count * bins_xl),
        2 * pairs, group_width, il_count * bins_il, xl_count * bins_xl,
    )


def solution(mesh):
    return jax.shard_map(
        per_device,
        mesh=mesh,
        in_specs=(
            P(("il", "xl"), None),
            P("il", "xl", None),
            P("il", "xl"),
            P(),
            P(),
            P(),
            P(),
            P("xl", None),
        ),
        out_specs=P("il", "xl", None, None),
        check_vma=False,
    )
```

```python
import functools

import jax
import jax.numpy as jnp
import numpy as np
from jax import lax
from jax.experimental import pallas as pl
from jax.experimental.pallas import tpu as pltpu
from jax.sharding import PartitionSpec as P


def window_first_weights(conv1_w, window):
    l_index = jnp.arange(window, dtype=jnp.int32)[None, :, None, None]
    c_index = jnp.arange(9, dtype=jnp.int32)[:, None, None, None]
    u_index = jnp.arange(4, dtype=jnp.int32)[None, None, :, None]
    tap_index = jnp.arange(8, dtype=jnp.int32)[None, None, None, :]
    start = jnp.where(c_index < 8, 16 * c_index + 12, -4)
    selector = (l_index - start - 4 * u_index == tap_index).astype(jnp.float32)
    return (
        jnp.einsum("clut,to->cluo", selector, conv1_w.astype(jnp.float32))
        .astype(jnp.bfloat16)
        .reshape(9, window, 4 * conv1_w.shape[1])
    )


MESH = pl.DeviceIdType.MESH


def exchange_kernel(n_il, n_xl, x_ref, y_ref, send_sem, recv_sem):
    n = n_il * n_xl
    me = lax.axis_index("il") * n_xl + lax.axis_index("xl")
    barrier = pltpu.get_barrier_semaphore()

    def greet(k, carry):
        d = lax.rem(me + 1 + k, n)
        pl.semaphore_signal(barrier, inc=1, device_id=(d // n_xl, d % n_xl), device_id_type=MESH)
        return carry

    lax.fori_loop(0, n - 1, greet, 0)
    pl.semaphore_wait(barrier, n - 1)
    pltpu.make_async_copy(x_ref.at[me], y_ref.at[me], recv_sem).start()

    def send(k, carry):
        d = lax.rem(me + 1 + k, n)
        pltpu.make_async_remote_copy(
            src_ref=x_ref.at[d], dst_ref=y_ref.at[me], send_sem=send_sem, recv_sem=recv_sem,
            device_id=(d // n_xl, d % n_xl), device_id_type=MESH,
        ).start()
        return carry

    lax.fori_loop(0, n - 1, send, 0)
    pltpu.make_async_copy(y_ref, y_ref, recv_sem).wait()
    pltpu.make_async_copy(x_ref.at[pl.ds(0, n - 1)], y_ref.at[pl.ds(0, n - 1)], send_sem).wait()


def exchange(x, n_il, n_xl, collective_id):
    return pl.pallas_call(
        functools.partial(exchange_kernel, n_il, n_xl),
        out_shape=jax.ShapeDtypeStruct(x.shape, x.dtype),
        in_specs=[pl.BlockSpec(memory_space=pl.ANY)],
        out_specs=pl.BlockSpec(memory_space=pl.ANY),
        scratch_shapes=[pltpu.SemaphoreType.DMA(()), pltpu.SemaphoreType.DMA(())],
        compiler_params=pltpu.CompilerParams(collective_id=collective_id, has_side_effects=True),
    )(x)

def encoder_kernel(n_il, n_xl, bins, arrived_ref, select_ref, counts_ref, b1_hbm, w2_hbm, w3_hbm,
                   w4_hbm, out_ref, stacked, paired, first_pad, second_pad, third_pad,
                   b1_ref, w2_ref, w3_ref, w4_ref, weight_sems):
    loads = [
        pltpu.make_async_copy(src, dst, weight_sems.at[i])
        for i, (src, dst) in enumerate(
            ((b1_hbm, b1_ref), (w2_hbm, w2_ref), (w3_hbm, w3_ref), (w4_hbm, w4_ref)))
    ]
    for load in loads:
        load.start()
    samples = arrived_ref.shape[1]
    width = w2_ref.shape[1]
    rows = first_pad.shape[0] - bins
    chunk = 8 * bins
    n_chunks = rows // chunk
    pair_rows = 2 * bins
    group = width // n_xl
    pairs_per_slab = out_ref.shape[2]
    blocks = samples // 128
    f32 = jnp.float32

    zeros_pad = jnp.zeros((bins, width), jnp.bfloat16)
    first_pad[pl.ds(0, bins), :] = zeros_pad
    second_pad[pl.ds(0, bins), :] = zeros_pad
    second_pad[pl.ds(bins + rows, bins), :] = zeros_pad
    third_pad[pl.ds(0, bins), :] = zeros_pad
    third_pad[pl.ds(bins + rows, bins), :] = zeros_pad

    counts = counts_ref[...]
    running = jnp.dot(select_ref[...], arrived_ref[...], preferred_element_type=f32)
    stacked[:, pl.ds(0, samples)] = (running / counts.astype(f32)).astype(jnp.bfloat16)
    stacked[:, pl.ds(samples, 128)] = jnp.zeros((bins, 128), jnp.bfloat16)
    for m in range(blocks):
        paired[pl.ds(m * bins, bins), :] = stacked[:, pl.ds(m * 128, 256)]

    def gelu(x):
        half = 0.5 * x
        inner = x * (np.float32(np.sqrt(2.0 / np.pi)) + np.float32(np.sqrt(2.0 / np.pi) * 0.044715) * (x * x))
        return half + half * jnp.tanh(inner)

    def layer1(c, carry):
        y = jnp.dot(paired[...], b1_ref[c], preferred_element_type=f32)
        y = gelu(y).astype(jnp.bfloat16)
        for m in range(blocks):
            step = 1 + c + 8 * m
            if m == blocks - 1:
                @pl.when(c < 7)
                def _():
                    first_pad[pl.ds(pl.multiple_of(bins + bins * step, bins), bins), :] = (
                        y[m * bins:(m + 1) * bins])
            else:
                first_pad[pl.ds(pl.multiple_of(bins + bins * step, bins), bins), :] = (
                    y[m * bins:(m + 1) * bins])
        return carry

    loads[0].wait()
    lax.fori_loop(0, 8, layer1, 0)
    y0 = jnp.dot(paired[pl.ds(0, bins), :], b1_ref[8], preferred_element_type=f32)
    first_pad[pl.ds(bins, bins), :] = gelu(y0).astype(jnp.bfloat16)

    def layer2(ci, carry):
        r0 = pl.multiple_of(ci * chunk, chunk)
        earlier = first_pad[pl.ds(r0, chunk), :]
        current = first_pad[pl.ds(r0 + bins, chunk), :]
        y = jnp.dot(earlier, w2_ref[pl.ds(0, width), :], preferred_element_type=f32)
        y = y + jnp.dot(current, w2_ref[pl.ds(width, width), :], preferred_element_type=f32)
        second_pad[pl.ds(bins + r0, chunk), :] = gelu(y).astype(jnp.bfloat16)
        return carry

    loads[1].wait()
    lax.fori_loop(0, n_chunks, layer2, 0)

    def centred(src, w_ref, r0):
        y = jnp.dot(src[pl.ds(r0, chunk), :], w_ref[pl.ds(0, width), :], preferred_element_type=f32)
        y = y + jnp.dot(src[pl.ds(r0 + bins, chunk), :], w_ref[pl.ds(width, width), :],
                        preferred_element_type=f32)
        y = y + jnp.dot(src[pl.ds(r0 + 2 * bins, chunk), :], w_ref[pl.ds(2 * width, width), :],
                        preferred_element_type=f32)
        return y

    def layer3(ci, carry):
        r0 = pl.multiple_of(ci * chunk, chunk)
        y = centred(second_pad, w3_ref, r0)
        third_pad[pl.ds(bins + r0, chunk), :] = gelu(y).astype(jnp.bfloat16)
        return carry

    loads[2].wait()
    lax.fori_loop(0, n_chunks, layer3, 0)

    def layer4(ci, carry):
        r0 = pl.multiple_of(ci * chunk, chunk)
        y = centred(third_pad, w4_ref, r0)
        y = y + second_pad[pl.ds(bins + r0, chunk), :].astype(f32)
        feat = y.astype(jnp.bfloat16).astype(f32)
        for p in range(chunk // pair_rows):
            pair = ci * (chunk // pair_rows) + p
            slab = pair // pairs_per_slab
            within = pair % pairs_per_slab
            block = feat[p * pair_rows:(p + 1) * pair_rows, :].T
            out_ref[slab, :, within, :, :] = block.reshape(n_xl, group, pair_rows).astype(
                jnp.bfloat16)
        return carry

    loads[3].wait()
    lax.fori_loop(0, n_chunks, layer4, 0)


def encode_to_send(arrived, select, counts, b1, conv2_w, conv3_w, conv4_w, n_il, n_xl):
    bins = select.shape[0]
    samples = arrived.shape[1]
    steps = samples // 16
    rows = steps * bins
    width = conv2_w.shape[1]
    out_shape = jax.ShapeDtypeStruct(
        (n_il, n_xl, steps // n_il // 2, width // n_xl, 2 * bins), jnp.bfloat16)
    return pl.pallas_call(
        functools.partial(encoder_kernel, n_il, n_xl, bins),
        out_shape=out_shape,
        in_specs=[pl.BlockSpec(memory_space=pltpu.VMEM)] * 3 + [pl.BlockSpec(memory_space=pl.ANY)] * 4,
        out_specs=pl.BlockSpec(memory_space=pltpu.VMEM),
        scratch_shapes=[
            pltpu.VMEM((bins, samples + 128), jnp.bfloat16),
            pltpu.VMEM((samples // 128 * bins, 256), jnp.bfloat16),
            pltpu.VMEM((bins + rows, width), jnp.bfloat16),
            pltpu.VMEM((2 * bins + rows, width), jnp.bfloat16),
            pltpu.VMEM((2 * bins + rows, width), jnp.bfloat16),
            pltpu.VMEM(b1.shape, b1.dtype),
            pltpu.VMEM(conv2_w.shape, conv2_w.dtype),
            pltpu.VMEM(conv3_w.shape, conv3_w.dtype),
            pltpu.VMEM(conv4_w.shape, conv4_w.dtype),
            pltpu.SemaphoreType.DMA((4,)),
        ],
        compiler_params=pltpu.CompilerParams(vmem_limit_bytes=48 * 1024 * 1024),
    )(arrived, select, counts, b1, conv2_w, conv3_w, conv4_w)


def merge_selectors(n_xl, lanes):
    width = lanes // n_xl
    kk = jnp.arange(2 * lanes, dtype=jnp.int32)[None, :, None]
    m = jnp.arange(n_xl * lanes, dtype=jnp.int32)[None, None, :]
    bp = jnp.arange(n_xl // 2, dtype=jnp.int32)[:, None, None]
    b = 2 * bp + kk // lanes
    lane = kk % lanes
    target = (lane // width) * lanes + width * b + lane % width
    return (m == target).astype(jnp.bfloat16)


def lane_tap_matrices(weight, lanes):
    offset = jnp.arange(lanes)[:, None] - jnp.arange(lanes)[None, :] + 1
    taps = weight.reshape(weight.shape[0], 3, 3, 1, 1)
    picked = jnp.zeros((weight.shape[0], 3, lanes, lanes), jnp.float32)
    for c in range(3):
        picked = picked + jnp.where(offset == c, taps[:, :, c], jnp.float32(0.0))
    high = lax.reduce_precision(picked, exponent_bits=8, mantissa_bits=7)
    low = (picked - high).astype(jnp.bfloat16)
    return jnp.stack([high.astype(jnp.bfloat16), low], axis=2)


def receive_kernel(recv_ref, sel_ref, taps_hbm, out_ref, field, taps_ref, taps_sem):
    taps_load = pltpu.make_async_copy(taps_hbm, taps_ref, taps_sem)
    taps_load.start()
    n_a, n_b, rows_k_o, lanes = recv_ref.shape
    n_s, n_o, n_p, n_q = out_ref.shape
    n_k = rows_k_o // n_o
    n_p4 = n_p // n_a
    per_o = n_s * n_p
    f32 = jnp.float32

    def merge(a, carry):
        y = None
        for bp in range(n_b // 2):
            x = jnp.concatenate([recv_ref[a, 2 * bp], recv_ref[a, 2 * bp + 1]], axis=1)
            d = jnp.dot(x, sel_ref[bp], preferred_element_type=f32)
            y = d if y is None else y + d
        for k in range(n_k):
            for s2 in range(2):
                for p4 in range(n_p4):
                    blk = y[k * n_o:(k + 1) * n_o, (s2 * n_p4 + p4) * lanes:(s2 * n_p4 + p4 + 1) * lanes]
                    start = (2 * k + s2) * n_p + n_p4 * a + p4
                    field[pl.ds(start, n_o, stride=per_o), :] = blk
        return carry

    lax.fori_loop(0, n_a, merge, 0)

    row = lax.broadcasted_iota(jnp.int32, (per_o, n_q), 0) % n_p
    zero = jnp.zeros((per_o, n_q), f32)

    def mix(o, carry):
        f = field[pl.ds(pl.multiple_of(o * per_o, per_o), per_o), :]
        fb = f.astype(jnp.bfloat16)
        g = []
        for r in range(3):
            t = jnp.dot(fb, taps_ref[o, r, 0], preferred_element_type=f32)
            t = t + jnp.dot(fb, taps_ref[o, r, 1], preferred_element_type=f32)
            g.append(t)
        acc = f + g[1]
        acc = acc + jnp.where(row == 0, zero, pltpu.roll(g[0], 1, 0))
        acc = acc + jnp.where(row == n_p - 1, zero, pltpu.roll(g[2], per_o - 1, 0))
        out_ref[:, o] = acc.astype(out_ref.dtype).reshape(n_s, n_p, n_q)
        return carry

    taps_load.wait()
    lax.fori_loop(0, n_o, mix, 0)


def receive_mix(received, sel, lw, n_s, n_o, n_p, n_q):
    return pl.pallas_call(
        receive_kernel,
        out_shape=jax.ShapeDtypeStruct((n_s, n_o, n_p, n_q), jnp.bfloat16),
        in_specs=[pl.BlockSpec(memory_space=pltpu.VMEM)] * 2 + [pl.BlockSpec(memory_space=pl.ANY)],
        out_specs=pl.BlockSpec(memory_space=pltpu.VMEM),
        scratch_shapes=[
            pltpu.VMEM((n_s * n_o * n_p, n_q), jnp.float32),
            pltpu.VMEM(lw.shape, lw.dtype),
            pltpu.SemaphoreType.DMA(()),
        ],
        compiler_params=pltpu.CompilerParams(vmem_limit_bytes=48 * 1024 * 1024),
    )(received, sel, lw)


def per_device(traces, fold_ids, fold_counts, conv1_w, conv2_w, conv3_w, conv4_w, lateral_w):
    il_count = lax.axis_size("il")
    xl_count = lax.axis_size("xl")
    devices = il_count * xl_count
    rows_here = traces.shape[0]
    samples = traces.shape[1]
    bins_il, bins_xl, fold_depth = fold_ids.shape
    bin_total = bins_il * bins_xl
    slot_total = bin_total * fold_depth
    capacity = 2 * slot_total // devices
    flat_ids = fold_ids.reshape(slot_total)
    source = flat_ids // rows_here
    local_row = flat_ids % rows_here
    onehot = (source[:, None] == jnp.arange(devices, dtype=jnp.int32)[None, :]).astype(jnp.int32)
    slot_rank = jnp.sum(onehot * jnp.cumsum(onehot, axis=0), axis=1) - 1
    position = source * capacity + slot_rank
    requests = (
        jnp.zeros((devices * capacity,), jnp.int32)
        .at[position]
        .set(local_row, mode="promise_in_bounds", unique_indices=True)
        .reshape(devices, capacity)
    )
    wanted = exchange(requests, il_count, xl_count, 1)
    picked = jnp.take(traces, wanted, axis=0, mode="clip")
    arrived = lax.all_to_all(picked, ("il", "xl"), split_axis=0, concat_axis=0, tiled=True)
    arrived = arrived.reshape(devices * capacity, samples)
    live = jnp.arange(fold_depth, dtype=jnp.int32)[None, :] < fold_counts.reshape(bin_total, 1)
    rows_in = jnp.arange(devices * capacity, dtype=jnp.int32)[None, None, :]
    select = jnp.any(
        (position.reshape(bin_total, fold_depth)[:, :, None] == rows_in) & live[:, :, None], axis=1
    ).astype(jnp.bfloat16)
    outgoing = encode_to_send(
        arrived, select, fold_counts.reshape(bin_total, 1), window_first_weights(conv1_w, 256),
        conv2_w, conv3_w, conv4_w, il_count, xl_count,
    )
    pairs = outgoing.shape[2]
    group_width = outgoing.shape[3]
    outgoing = outgoing.reshape(devices, pairs, group_width, 2 * bin_total)
    received = lax.all_to_all(outgoing, ("il", "xl"), split_axis=0, concat_axis=0, tiled=True)
    received = received.reshape(il_count, xl_count, pairs * group_width, 2 * bin_total)
    return receive_mix(
        received, merge_selectors(xl_count, 2 * bin_total),
        lane_tap_matrices(lateral_w, xl_count * bins_xl),
        2 * pairs, group_width, il_count * bins_il, xl_count * bins_xl,
    )


def solution(mesh):
    return jax.shard_map(
        per_device,
        mesh=mesh,
        in_specs=(
            P(("il", "xl"), None),
            P("il", "xl", None),
            P("il", "xl"),
            P(),
            P(),
            P(),
            P(),
            P("xl", None),
        ),
        out_specs=P("il", "xl", None, None),
        check_vma=False,
    )
```
